512 devices in a mesh: member: 16 (over z), patch: 32 (over y, x, core).
Axes of the slice: x: 4, y: 4, z: 16, core: 2. Of those that a mesh axis runs over, the one named last changes fastest.
Arguments:
- ensemble: bfloat16 [16, 8192, 512], P('member', 'patch'), may hold values from -6 to 6
- forcing: bfloat16 [16, 8192, 512], P('member', 'patch'), may hold values from -6 to 6
- clone_before: int32 [16], replicated, may hold values from 0 to 15
- clone_after: int32 [16], replicated, may hold values from 0 to 15
- link_mask: int32 [64, 8], P('patch'), may hold values 0 or 1
- attn_gain: float32 [512], replicated, may hold values from 0.25 to 1.75
- w_query: bfloat16 [512, 512], replicated, may hold values from -32 to 32
- w_key: bfloat16 [512, 512], replicated, may hold values from -1 to 1
- w_value: bfloat16 [512, 512], replicated, may hold values from -0.25 to 0.25
- w_out: bfloat16 [512, 512], replicated, may hold values from -0.25 to 0.25
- mlp_gain: float32 [512], replicated, may hold values from 0.25 to 1.75
- w_up: bfloat16 [512, 1024], replicated, may hold values from -0.25 to 0.25
- w_down: bfloat16 [1024, 512], replicated, may hold values from -0.1875 to 0.1875
Outputs:
- advanced: bfloat16 [16, 8192, 512], P('member', 'patch')
The draws below stay inside these ranges and needn't reach their ends.
All inputs are finite; a program needn't handle non-finite values. No bound on the sum of `link_mask` on one device may be relied on, other than what follows from the above.
Results may differ from the reference program's by a relative error of at most 0.006.
Values may be sent and summed in bfloat16 or wider, within the bound.
A program may use at most 64 MiB of HBM per device.

```python
import jax
import jax.numpy as jnp
from jax import lax

D = 512
HEADS = 4
FF = 1024
BLOCK = 128
REACH = 4
HEAD = 128
MEMBERS = 16
NODES = 8192
NBLOCKS = 64


def weight_pair(key):
    key_first = jax.random.fold_in(key, 11)
    key_second = jax.random.fold_in(key, 12)
    spread = jnp.float32(D) ** (-0.5)
    key_weights = jnp.clip(jax.random.normal(key_first, (D, D), jnp.float32), -6.0, 6.0) * spread
    query_weights = jnp.clip(jax.random.normal(key_second, (D, D), jnp.float32), -6.0, 6.0) * spread
    return (query_weights, key_weights)


def draw_w_query(key, part):
    return weight_pair(key)[0].astype(jnp.bfloat16)


def draw_w_key(key, part):
    return weight_pair(key)[1].astype(jnp.bfloat16)


def plant(result, key, smallest, largest):
    index_at = [jax.random.randint(jax.random.fold_in(key, axis), (), 0, length) for axis, length in enumerate(result.shape)]
    main_axis = result.shape.index(max(result.shape))
    neighbour = index_at[:main_axis] + [(index_at[main_axis] + 1) % result.shape[main_axis]] + index_at[main_axis + 1:]
    return result.at[tuple(index_at)].set(smallest).at[tuple(neighbour)].set(largest)


def levels(own_key, dims, shards, least, top_value):
    def one(position, parts):
        draws = jax.random.uniform(jax.random.fold_in(jax.random.fold_in(own_key, 6), position), (parts,), jnp.float32, least / len(shards), top_value / len(shards))
        return jnp.repeat(jnp.exp(draws), dims[position] // parts).reshape((-1,) + (1,) * (len(dims) - position - 1))

    level = one(*shards[0])
    for cut in shards[1:]:
        level = level * one(*cut)
    return level


def gaussian(own_key, dims, scale, reach, shards=(), held_as=jnp.bfloat16):
    entries = jax.random.normal(own_key, dims, jnp.float32) * scale
    if len(shards) > 0:
        entries = levels(own_key, dims, shards, -0.22, 0.18) * entries
    return jnp.clip(entries, min=-reach, max=reach).astype(held_as)


def setup_inputs(seed: int = 0) -> dict:
    arg_keys = jax.random.split(jax.random.key(seed), 14)
    return {
        "ensemble": gaussian(arg_keys[0], (MEMBERS, NODES, D), 1.0, 6.0, ((0, 16), (1, 32))),
        "forcing": gaussian(arg_keys[1], (MEMBERS, NODES, D), 1.0, 6.0, ((0, 16), (1, 32))),
        "clone_before": plant(jax.random.randint(arg_keys[2], (MEMBERS,), 0, MEMBERS), jax.random.fold_in(arg_keys[2], 1), 0, MEMBERS - 1).astype(jnp.int32),
        "clone_after": plant(jax.random.randint(arg_keys[3], (MEMBERS,), 0, MEMBERS), jax.random.fold_in(arg_keys[3], 1), 0, MEMBERS - 1).astype(jnp.int32),
        "link_mask": plant((jax.random.randint(arg_keys[4], (NBLOCKS, 2 * REACH), 0, 4) < 3).astype(jnp.int32), jax.random.fold_in(arg_keys[4], 1), 0, 1),
        "attn_gain": jnp.clip(1.0 + 0.15 * jax.random.normal(arg_keys[5], (D,), jnp.float32), 0.25, 1.75),
        "w_query": draw_w_query(jax.random.fold_in(arg_keys[13], 71), 0),
        "w_key": draw_w_key(jax.random.fold_in(arg_keys[13], 71), 0),
        "w_value": gaussian(arg_keys[8], (D, D), D ** -0.5, 0.25),
        "w_out": gaussian(arg_keys[9], (D, D), D ** -0.5, 0.25),
        "mlp_gain": jnp.clip(1.0 + 0.15 * jax.random.normal(arg_keys[10], (D,), jnp.float32), 0.25, 1.75),
        "w_up": gaussian(arg_keys[11], (D, FF), D ** -0.5, 0.25),
        "w_down": gaussian(arg_keys[12], (FF, D), FF ** -0.5, 0.1875),
    }


def rms_norm(values, gain):
    scale = lax.rsqrt(lax.optimization_barrier(jnp.mean(values * values, axis=-1, keepdims=True)) + 1e-06)
    return (values * scale * gain).astype(jnp.bfloat16)

def drift(member, link_mask, attn_gain, w_query, w_key, w_value, w_out, mlp_gain, w_up, w_down):
    blocks = NODES // BLOCK
    normed = rms_norm(member.astype(jnp.float32), attn_gain)
    queries = jnp.dot(normed, w_query, preferred_element_type=jnp.float32).astype(jnp.bfloat16)
    key_rows = jnp.dot(normed, w_key, preferred_element_type=jnp.float32).astype(jnp.bfloat16)
    value_rows = jnp.dot(normed, w_value, preferred_element_type=jnp.float32).astype(jnp.bfloat16)
    query_blocks = queries.reshape(blocks, BLOCK, HEADS, HEAD)
    key_blocks = key_rows.reshape(blocks, BLOCK, HEADS, HEAD)
    value_blocks = value_rows.reshape(blocks, BLOCK, HEADS, HEAD)
    key_list = []
    value_list = []
    mask_list = []
    for offset in range(-REACH, REACH + 1):
        key_list.append(jnp.roll(key_blocks, -offset, axis=0))
        value_list.append(jnp.roll(value_blocks, -offset, axis=0))
        if offset == 0:
            allowed = jnp.ones((blocks,), dtype=bool)
        else:
            column = offset + REACH if offset < 0 else offset + REACH - 1
            allowed = link_mask[:, column] > 0
        mask_list.append(jnp.broadcast_to(allowed[:, None], (blocks, BLOCK)))
    key_cat = jnp.concatenate(key_list, axis=1).astype(jnp.float32)
    value_cat = jnp.concatenate(value_list, axis=1).astype(jnp.float32)
    allowed = jnp.concatenate(mask_list, axis=1)[:, None, None, :]
    scores = jnp.einsum('bqhd,bkhd->bhqk', query_blocks.astype(jnp.float32), key_cat) / jnp.sqrt(jnp.float32(HEAD))
    scores = jnp.where(allowed, scores, -jnp.inf)
    highest = lax.optimization_barrier(jnp.max(scores, axis=-1, keepdims=True))
    expd = jnp.exp(scores - highest)
    weights = (expd / lax.optimization_barrier(jnp.sum(expd, axis=-1, keepdims=True))).astype(jnp.bfloat16)
    mixed = jnp.einsum('bhqk,bkhd->bqhd', weights.astype(jnp.float32), value_cat).astype(jnp.bfloat16)
    attended = jnp.dot(mixed.reshape(NODES, D), w_out, preferred_element_type=jnp.float32)
    lifted = member.astype(jnp.float32) + attended
    hidden = jax.nn.gelu(jnp.dot(rms_norm(lifted, mlp_gain), w_up, preferred_element_type=jnp.float32), approximate=True).astype(jnp.bfloat16)
    return (attended + jnp.dot(hidden, w_down, preferred_element_type=jnp.float32)).astype(jnp.bfloat16)

def reference(ensemble, forcing, clone_before, clone_after, link_mask, attn_gain, w_query, w_key, w_value, w_out, mlp_gain, w_up, w_down):
    start = jnp.take(ensemble, clone_before.astype(jnp.int32), axis=0)

    def advance(pair):
        member, noise = pair
        first = drift(member, link_mask, attn_gain, w_query, w_key, w_value, w_out, mlp_gain, w_up, w_down)
        guess = (member.astype(jnp.float32) + 0.5 * first.astype(jnp.float32) + 0.3 * noise.astype(jnp.float32)).astype(jnp.bfloat16)
        second = drift(guess, link_mask, attn_gain, w_query, w_key, w_value, w_out, mlp_gain, w_up, w_down)
        total = first.astype(jnp.float32) + second.astype(jnp.float32)
        return (member.astype(jnp.float32) + 0.25 * total + 0.3 * noise.astype(jnp.float32)).astype(jnp.bfloat16)
    stepped = lax.map(advance, (start, forcing))
    return jnp.take(stepped, clone_after.astype(jnp.int32), axis=0)
```

```python
import functools

import jax
import jax.numpy as jnp
from jax import lax
from jax.experimental import pallas as pl
from jax.experimental.pallas import tpu as pltpu
from jax.sharding import PartitionSpec as P

HEADS = 4
BLOCK = 128
REACH = 4
CHUNKS = 4
MESH = pl.DeviceIdType.MESH
BF = jnp.bfloat16
F32 = jnp.float32


def dot(a, b):
    return jnp.dot(a, b, preferred_element_type=F32)


def dot_nt(a, b):
    return lax.dot_general(a, b, (((1,), (1,)), ((), ())), preferred_element_type=F32)


def rms(x, gain):
    scale = lax.rsqrt(jnp.mean(x * x, axis=-1, keepdims=True) + 1e-06)
    return (x * scale * gain).astype(BF)


def gelu(x):
    return 0.5 * x * (1.0 + jnp.tanh(0.7978845608028654 * (x + 0.044715 * x * x * x)))


def kernel(members, patches, *refs):
    (cb, ca, mask, e_in, f_in, g1, g2, wq_in, wk_in, wv_in, wo_in, wu_in, wd_in, out) = refs[:14]
    scratch = list(refs[14:])
    zb = [[scratch.pop(0) for _ in range(CHUNKS)] for _ in range(2)]
    nb = [scratch.pop(0) for _ in range(2)]
    wq, wk, wv, wo, wu, wd = [scratch.pop(0) for _ in range(6)]
    kb, vb, qb, mb, st, first, att, fx = [scratch.pop(0) for _ in range(8)]
    w_sem, own_sem, z_send, z_recv, h_send, h_recv = scratch

    z = lax.axis_index("member")
    p = lax.axis_index("patch")
    nodes, width = st.shape
    rows = nodes // CHUNKS
    head = width // HEADS
    right_ages = members // 2
    left_ages = members - 1 - right_ages

    def dz(off):
        return {"member": lax.rem(z + off + members, members)}

    def dp(off):
        return {"patch": lax.rem(p + off + patches, patches)}

    w_copies = [
        pltpu.make_async_copy(s, d, w_sem.at[i])
        for i, (s, d) in enumerate(zip((wq_in, wk_in, wv_in, wo_in, wu_in, wd_in), (wq, wk, wv, wo, wu, wd)))
    ]
    own = [
        [
            pltpu.make_async_copy(src.at[0, pl.ds(c * rows, rows)], zb[g][c].at[0], own_sem.at[g, c])
            for c in range(CHUNKS)
        ]
        for g, src in enumerate((e_in, f_in))
    ]
    for g in range(2):
        for c in range(CHUNKS):
            own[g][c].start()
    for w in w_copies:
        w.start()

    barrier = pltpu.get_barrier_semaphore()
    peers = [dz(1), dz(-1), dp(1), dp(-1), dp(2), dp(-2)]
    for peer in peers:
        pl.semaphore_signal(barrier, inc=1, device_id=peer, device_id_type=MESH)
    pl.semaphore_wait(barrier, len(peers))

    def ring(g, c, way, age):
        if way == 0:
            src, dst = age, age + 1
        else:
            src, dst = lax.rem(members - age, members), members - 1 - age
        return pltpu.make_async_remote_copy(
            src_ref=zb[g][c].at[src],
            dst_ref=zb[g][c].at[dst],
            send_sem=z_send.at[g, c, way],
            recv_sem=z_recv.at[g, c, way, age],
            device_id=dz(1 if way == 0 else -1),
            device_id_type=MESH,
        )

    def z_first(g):
        for c in range(CHUNKS):
            own[g][c].wait()
            ring(g, c, 0, 0).start()
            ring(g, c, 1, 0).start()

    def z_step(g, age, chunks):
        for c in chunks:
            ring(g, c, 0, age - 1).wait_recv()
            ring(g, c, 0, age).start()
            ring(g, c, 1, age - 1).wait_recv()
            ring(g, c, 1, age).start()

    def z_last(g, chunks):
        for c in chunks:
            ring(g, c, 0, right_ages - 2).wait_recv()
            ring(g, c, 0, right_ages - 1).start()
            ring(g, c, 1, left_ages - 1).wait_recv()

    def z_end(g, c):
        ring(g, c, 0, right_ages - 1).wait_recv()

    def z_drain():
        for g in range(2):
            for c in range(CHUNKS):
                for way, ages in ((0, right_ages), (1, left_ages)):
                    part = zb[g][c].at[pl.ds(0, ages)]
                    pltpu.make_async_remote_copy(
                        src_ref=part,
                        dst_ref=part,
                        send_sem=z_send.at[g, c, way],
                        recv_sem=z_recv.at[g, c, way, 0],
                        device_id=dz(1 if way == 0 else -1),
                        device_id_type=MESH,
                    ).wait_send()

    def halo(k, off, c):
        part = pl.ds(c * rows, rows)
        return pltpu.make_async_remote_copy(
            src_ref=nb[k].at[2, part],
            dst_ref=nb[k].at[2 - off, part],
            send_sem=h_send.at[k, 2 - off, c],
            recv_sem=h_recv.at[k, 2 - off, c],
            device_id=dp(off),
            device_id_type=MESH,
        )

    offsets = (1, -1, 2, -2)

    def publish(k, c, x):
        part = pl.ds(c * rows, rows)
        nb[k][2, part] = rms(x.astype(F32), g1[...])
        for off in offsets:
            halo(k, off, c).start()

    def arrive(k, slot):
        for c in range(CHUNKS):
            halo(k, 2 - slot, c).wait_recv()

    def keys_values(k, slot):
        part = pl.ds(slot * nodes, nodes)
        src = nb[k][slot]
        ks = dot(src, wk[...]).astype(BF)
        vs = dot(src, wv[...]).astype(BF)
        for h in range(HEADS):
            kb[h, part] = ks[:, h * head : (h + 1) * head]
            vb[h, part] = vs[:, h * head : (h + 1) * head]

    def queries(k):
        qs = dot(nb[k][2], wq[...]).astype(BF)
        for h in range(HEADS):
            qb[h] = qs[:, h * head : (h + 1) * head]

    factor = 1.4426950408889634 / head**0.5
    span = 2 * REACH + 1

    def attend(b, h):
        kv = pl.ds(b * BLOCK, span * BLOCK)
        s = dot_nt(qb[h, pl.ds(b * BLOCK, BLOCK)], kb[h, kv]) * factor
        parts = []
        for i in range(span):
            piece = s[:, i * BLOCK : (i + 1) * BLOCK]
            if i != REACH:
                link = mask[b, i if i < REACH else i - 1]
                piece = piece + jnp.where(link > 0, F32(0.0), F32(-jnp.inf))
            parts.append(piece)
        s = jnp.concatenate(parts, axis=1)
        top = jnp.max(s, axis=1, keepdims=True)
        e = jnp.exp2(s - top)
        total = jnp.sum(e, axis=1, keepdims=True)
        mixed = dot(e.astype(BF), vb[h, kv]) / total
        mb[pl.ds(b * BLOCK, BLOCK), pl.ds(pl.multiple_of(h * head, head), head)] = mixed.astype(BF)

    def finish(state):
        att[...] = dot(mb[...], wo[...])
        lifted = state[...].astype(F32) + att[...]
        hidden = gelu(dot(rms(lifted, g2[...]), wu[...])).astype(BF)
        return (att[...] + dot(hidden, wd[...])).astype(BF)

    z_first(0)

    @pl.loop(1, left_ages)
    def _(age):
        z_step(0, age, range(CHUNKS))

    z_last(0, range(CHUNKS))
    z_first(1)

    d_e = lax.rem(z - cb[ca[z]] + members, members)
    d_f = lax.rem(z - ca[z] + members, members)
    for c in range(CHUNKS):
        z_end(0, c)
        part = pl.ds(c * rows, rows)
        x = zb[0][c][d_e]
        st[part] = x
        publish(0, c, x)
    for w in w_copies:
        w.wait()
    queries(0)
    keys_values(0, 2)
    z_step(1, 1, range(CHUNKS))
    for slot in (1, 3):
        arrive(0, slot)
        keys_values(0, slot)
    z_step(1, 2, range(CHUNKS))
    for slot in (0, 4):
        arrive(0, slot)
        keys_values(0, slot)

    half = CHUNKS // 2

    @pl.loop(0, HEADS)
    def _(h):
        attend(0, h)

        @pl.when(h < HEADS - 1)
        def _():
            z_step(1, 3 + h, range(half))

        attend(1, h)

        @pl.when(h < HEADS - 1)
        def _():
            z_step(1, 3 + h, range(half, CHUNKS))

    first[...] = finish(st)

    @pl.loop(3 + HEADS - 1, left_ages)
    def _(age):
        z_step(1, age, range(CHUNKS))

    z_last(1, range(CHUNKS))
    for c in range(CHUNKS):
        z_end(1, c)
        part = pl.ds(c * rows, rows)
        base = st[part].astype(F32) + 0.3 * zb[1][c][d_f].astype(F32)
        x = (base + 0.5 * first[part].astype(F32)).astype(BF)
        fx[part] = x
        publish(1, c, x)
    queries(1)
    keys_values(1, 2)
    for slot in (1, 3, 0, 4):
        arrive(1, slot)
        keys_values(1, slot)

    @pl.loop(0, HEADS)
    def _(h):
        attend(0, h)
        attend(1, h)

    second = finish(fx).astype(F32)
    for c in range(CHUNKS):
        part = pl.ds(c * rows, rows)
        base = st[part].astype(F32)
        tot = first[part].astype(F32) + second[c * rows : (c + 1) * rows]
        out[0, part] = (base + 0.25 * tot + 0.3 * zb[1][c][d_f].astype(F32)).astype(BF)

    for k in range(2):
        for off in offsets:
            for c in range(CHUNKS):
                halo(k, off, c).wait_send()
    z_drain()


def solution(mesh):
    members, patches = mesh.shape["member"], mesh.shape["patch"]

    def shards(ensemble, forcing, cb, ca, mask, g1, wq, wk, wv, wo, g2, wu, wd):
        _, nodes, width = ensemble.shape
        hidden = wu.shape[1]
        rows = nodes // CHUNKS
        head = width // HEADS
        smem = pl.BlockSpec(memory_space=pltpu.SMEM)
        vmem = pl.BlockSpec(memory_space=pltpu.VMEM)
        anym = pl.BlockSpec(memory_space=pl.ANY)
        return pl.pallas_call(
            functools.partial(kernel, members, patches),
            out_shape=jax.ShapeDtypeStruct(ensemble.shape, BF),
            in_specs=[smem] * 3 + [anym] * 2 + [vmem] * 2 + [anym] * 6,
            out_specs=vmem,
            scratch_shapes=[pltpu.VMEM((members, rows, width), BF) for _ in range(2 * CHUNKS)]
            + [pltpu.VMEM((5, nodes, width), BF) for _ in range(2)]
            + [pltpu.VMEM((width, width), BF) for _ in range(4)]
            + [pltpu.VMEM((width, hidden), BF), pltpu.VMEM((hidden, width), BF)]
            + [
                pltpu.VMEM((HEADS, 5 * nodes, head), BF),
                pltpu.VMEM((HEADS, 5 * nodes, head), BF),
                pltpu.VMEM((HEADS, nodes, head), BF),
                pltpu.VMEM((nodes, width), BF),
                pltpu.VMEM((nodes, width), BF),
                pltpu.VMEM((nodes, width), BF),
                pltpu.VMEM((nodes, width), F32),
                pltpu.VMEM((nodes, width), BF),
                pltpu.SemaphoreType.DMA((6,)),
                pltpu.SemaphoreType.DMA((2, CHUNKS)),
                pltpu.SemaphoreType.DMA((2, CHUNKS, 2)),
                pltpu.SemaphoreType.DMA((2, CHUNKS, 2, members // 2)),
                pltpu.SemaphoreType.DMA((2, 5, CHUNKS)),
                pltpu.SemaphoreType.DMA((2, 5, CHUNKS)),
            ],
            compiler_params=pltpu.CompilerParams(
                collective_id=0, has_side_effects=True, vmem_limit_bytes=56 * 1024 * 1024
            ),
            name="heun",
        )(cb, ca, mask, ensemble, forcing, g1.reshape(1, width), g2.reshape(1, width), wq, wk, wv, wo, wu, wd)

    placed = (P("member", "patch", None),) * 2 + (P(), P(), P("patch", None)) + (P(),) * 8
    return jax.shard_map(
        shards, mesh=mesh, in_specs=placed, out_specs=P("member", "patch", None), check_vma=False
    )
```

```python
import functools

import jax
import jax.numpy as jnp
from jax import lax
from jax.experimental import pallas as pl
from jax.experimental.pallas import tpu as pltpu
from jax.sharding import PartitionSpec as P

HEADS = 4
BLOCK = 128
REACH = 4
CHUNKS = 4
PIECES = 8
LAG = 4
HOPS = 10
PLANS = 64
MID = 48
STEPS = 72
MESH = pl.DeviceIdType.MESH
BF = jnp.bfloat16
F32 = jnp.float32


def dot(a, b):
    return jnp.dot(a, b, preferred_element_type=F32)


def dot_nt(a, b):
    return lax.dot_general(a, b, (((1,), (1,)), ((), ())), preferred_element_type=F32)


def rms(x, gain):
    scale = lax.rsqrt(jnp.mean(x * x, axis=-1, keepdims=True) + 1e-06)
    return (x * scale * gain).astype(BF)


def gelu(x):
    return 0.5 * x * (1.0 + jnp.tanh(0.7978845608028654 * (x + 0.044715 * x * x * x)))


def drift_tools(
    chunks, p, dp, mask, g1, g2, nb, wq, wk, wv, wo, wu, wd, kb, vb, qb, mb, att, h_send, h_recv
):
    _, nodes, width = nb[0].shape
    rows = nodes // chunks
    head = width // HEADS

    def halo(k, off, c):
        part = pl.ds(c * rows, rows)
        return pltpu.make_async_remote_copy(
            src_ref=nb[k].at[2, part],
            dst_ref=nb[k].at[2 - off, part],
            send_sem=h_send.at[k, 2 - off, c],
            recv_sem=h_recv.at[k, 2 - off, c],
            device_id=dp(off),
            device_id_type=MESH,
        )

    offsets = (1, -1, 2, -2)

    def publish(k, c, x):
        part = pl.ds(c * rows, rows)
        nb[k][2, part] = rms(x.astype(F32), g1[...])
        for off in offsets:
            halo(k, off, c).start()

    def arrive(k, slot):
        for c in range(chunks):
            halo(k, 2 - slot, c).wait_recv()

    def keys_values(k, slot):
        part = pl.ds(slot * nodes, nodes)
        src = nb[k][slot]
        ks = dot(src, wk[...]).astype(BF)
        vs = dot(src, wv[...]).astype(BF)
        for h in range(HEADS):
            kb[h, part] = ks[:, h * head : (h + 1) * head]
            vb[h, part] = vs[:, h * head : (h + 1) * head]

    def queries(k):
        qs = dot(nb[k][2], wq[...]).astype(BF)
        for h in range(HEADS):
            qb[h] = qs[:, h * head : (h + 1) * head]

    factor = 1.4426950408889634 / head**0.5
    span = 2 * REACH + 1

    def attend(b, h):
        kv = pl.ds(b * BLOCK, span * BLOCK)
        s = dot_nt(qb[h, pl.ds(b * BLOCK, BLOCK)], kb[h, kv]) * factor
        parts = []
        for i in range(span):
            piece = s[:, i * BLOCK : (i + 1) * BLOCK]
            if i != REACH:
                link = mask[b, i if i < REACH else i - 1]
                piece = piece + jnp.where(link > 0, F32(0.0), F32(-jnp.inf))
            parts.append(piece)
        s = jnp.concatenate(parts, axis=1)
        top = jnp.max(s, axis=1, keepdims=True)
        e = jnp.exp2(s - top)
        total = jnp.sum(e, axis=1, keepdims=True)
        mixed = dot(e.astype(BF), vb[h, kv]) / total
        mb[pl.ds(b * BLOCK, BLOCK), pl.ds(pl.multiple_of(h * head, head), head)] = mixed.astype(BF)

    def finish(state):
        att[...] = dot(mb[...], wo[...])
        lifted = state[...].astype(F32) + att[...]
        hidden = gelu(dot(rms(lifted, g2[...]), wu[...])).astype(BF)
        return (att[...] + dot(hidden, wd[...])).astype(BF)

    def h_drain():
        for k in range(2):
            for off in offsets:
                for c in range(chunks):
                    halo(k, off, c).wait_send()

    return publish, arrive, keys_values, queries, attend, finish, h_drain


def ring_kernel(members, patches, *refs):
    (cb, ca, mask, e_in, f_in, g1, g2, wq_in, wk_in, wv_in, wo_in, wu_in, wd_in, out) = refs[:14]
    scratch = list(refs[14:])
    zb = [[scratch.pop(0) for _ in range(CHUNKS)] for _ in range(2)]
    nb = [scratch.pop(0) for _ in range(2)]
    wq, wk, wv, wo, wu, wd = [scratch.pop(0) for _ in range(6)]
    kb, vb, qb, mb, st, first, att, fx = [scratch.pop(0) for _ in range(8)]
    w_sem, own_sem, z_send, z_recv, h_send, h_recv = scratch

    z = lax.axis_index("member")
    p = lax.axis_index("patch")
    nodes, width = st.shape
    rows = nodes // CHUNKS
    head = width // HEADS
    right_ages = members // 2
    left_ages = members - 1 - right_ages

    def dz(off):
        return {"member": lax.rem(z + off + members, members)}

    def dp(off):
        return {"patch": lax.rem(p + off + patches, patches)}

    w_copies = [
        pltpu.make_async_copy(s, d, w_sem.at[i])
        for i, (s, d) in enumerate(zip((wq_in, wk_in, wv_in, wo_in, wu_in, wd_in), (wq, wk, wv, wo, wu, wd)))
    ]
    own = [
        [
            pltpu.make_async_copy(src.at[0, pl.ds(c * rows, rows)], zb[g][c].at[0], own_sem.at[g, c])
            for c in range(CHUNKS)
        ]
        for g, src in enumerate((e_in, f_in))
    ]
    for g in range(2):
        for c in range(CHUNKS):
            own[g][c].start()
    for w in w_copies:
        w.start()

    barrier = pltpu.get_barrier_semaphore()
    peers = [dz(1), dz(-1), dp(1), dp(-1), dp(2), dp(-2)]
    for peer in peers:
        pl.semaphore_signal(barrier, inc=1, device_id=peer, device_id_type=MESH)
    pl.semaphore_wait(barrier, len(peers))

    def ring(g, c, way, age):
        if way == 0:
            src, dst = age, age + 1
        else:
            src, dst = lax.rem(members - age, members), members - 1 - age
        return pltpu.make_async_remote_copy(
            src_ref=zb[g][c].at[src],
            dst_ref=zb[g][c].at[dst],
            send_sem=z_send.at[g, c, way],
            recv_sem=z_recv.at[g, c, way, age],
            device_id=dz(1 if way == 0 else -1),
            device_id_type=MESH,
        )

    def z_first(g):
        for c in range(CHUNKS):
            own[g][c].wait()
            ring(g, c, 0, 0).start()
            ring(g, c, 1, 0).start()

    def z_step(g, age, chunks):
        for c in chunks:
            ring(g, c, 0, age - 1).wait_recv()
            ring(g, c, 0, age).start()
            ring(g, c, 1, age - 1).wait_recv()
            ring(g, c, 1, age).start()

    def z_last(g, chunks):
        for c in chunks:
            ring(g, c, 0, right_ages - 2).wait_recv()
            ring(g, c, 0, right_ages - 1).start()
            ring(g, c, 1, left_ages - 1).wait_recv()

    def z_end(g, c):
        ring(g, c, 0, right_ages - 1).wait_recv()

    def z_drain():
        for g in range(2):
            for c in range(CHUNKS):
                for way, ages in ((0, right_ages), (1, left_ages)):
                    part = zb[g][c].at[pl.ds(0, ages)]
                    pltpu.make_async_remote_copy(
                        src_ref=part,
                        dst_ref=part,
                        send_sem=z_send.at[g, c, way],
                        recv_sem=z_recv.at[g, c, way, 0],
                        device_id=dz(1 if way == 0 else -1),
                        device_id_type=MESH,
                    ).wait_send()

    publish, arrive, keys_values, queries, attend, finish, h_drain = drift_tools(
        CHUNKS, p, dp, mask, g1, g2, nb, wq, wk, wv, wo, wu, wd, kb, vb, qb, mb, att, h_send, h_recv
    )

    z_first(0)

    @pl.loop(1, left_ages)
    def _(age):
        z_step(0, age, range(CHUNKS))

    z_last(0, range(CHUNKS))
    z_first(1)

    d_e = lax.rem(z - cb[ca[z]] + members, members)
    d_f = lax.rem(z - ca[z] + members, members)
    for c in range(CHUNKS):
        z_end(0, c)
        part = pl.ds(c * rows, rows)
        x = zb[0][c][d_e]
        st[part] = x
        publish(0, c, x)
    for w in w_copies:
        w.wait()
    queries(0)
    keys_values(0, 2)
    z_step(1, 1, range(CHUNKS))
    for slot in (1, 3):
        arrive(0, slot)
        keys_values(0, slot)
    z_step(1, 2, range(CHUNKS))
    for slot in (0, 4):
        arrive(0, slot)
        keys_values(0, slot)

    half = CHUNKS // 2

    @pl.loop(0, HEADS)
    def _(h):
        attend(0, h)

        @pl.when(h < HEADS - 1)
        def _():
            z_step(1, 3 + h, range(half))

        attend(1, h)

        @pl.when(h < HEADS - 1)
        def _():
            z_step(1, 3 + h, range(half, CHUNKS))

    first[...] = finish(st)

    @pl.loop(3 + HEADS - 1, left_ages)
    def _(age):
        z_step(1, age, range(CHUNKS))

    z_last(1, range(CHUNKS))
    for c in range(CHUNKS):
        z_end(1, c)
        part = pl.ds(c * rows, rows)
        base = st[part].astype(F32) + 0.3 * zb[1][c][d_f].astype(F32)
        x = (base + 0.5 * first[part].astype(F32)).astype(BF)
        fx[part] = x
        publish(1, c, x)
    queries(1)
    keys_values(1, 2)
    for slot in (1, 3, 0, 4):
        arrive(1, slot)
        keys_values(1, slot)

    @pl.loop(0, HEADS)
    def _(h):
        attend(0, h)
        attend(1, h)

    second = finish(fx).astype(F32)
    for c in range(CHUNKS):
        part = pl.ds(c * rows, rows)
        base = st[part].astype(F32)
        tot = first[part].astype(F32) + second[c * rows : (c + 1) * rows]
        out[0, part] = (base + 0.25 * tot + 0.3 * zb[1][c][d_f].astype(F32)).astype(BF)

    h_drain()
    z_drain()


def thresholds(shape, members, g):
    q = lax.broadcasted_iota(jnp.int32, shape, 0)
    s = lax.rem(lax.broadcasted_iota(jnp.int32, shape, 1), members)
    x = (q * 40503 + s * 30011 + (g * 12289 + 7)) & 0xFFFF
    x = (x * 25173 + 13849) & 0xFFFF
    x = x ^ (x >> 7)
    x = (x * 25173 + 13849) & 0xFFFF
    x = x ^ (x >> 9)
    half = members // 2
    low = members - HOPS
    wide = low + ((x * (HOPS - low + 1)) >> 16)
    near = half - 1 + ((x * 2) >> 16)
    return jnp.where(q == 0, half, jnp.where(q == 1, half - 1, jnp.where(q < shape[0] // 4, near, wide)))


def make_plan(members, z, sources, starts, plan):
    shape = starts.shape[2:]
    lane = lax.broadcasted_iota(jnp.int32, shape, 1)
    slot = lax.rem(lane, members)
    zero = jnp.zeros(shape, jnp.int32)
    reach = []
    for g in range(2):
        src = zero
        for m in range(members):
            src = jnp.where(slot == m, sources[g][m], src)
        dist = lax.rem(slot - src + members, members)
        right = dist <= thresholds(shape, members, g)
        away = (jnp.where(right, dist, 0), jnp.where(right, 0, members - dist))
        both = []
        for way in range(2):
            far = zero
            for b in range(1, HOPS + 1):
                shift = (128 - b) if way == 0 else b
                far = jnp.where(pltpu.roll(away[way], shift, 1) == b, b, far)
            both.append(far)
        reach.append(both)
    free = [zero, zero]
    ends = []
    for g in range(2):
        before = [None, None]
        for a in range(HOPS):
            for way in range(2):
                sgn = 1 if way == 0 else 127
                far = reach[g][way]
                if a > 0:
                    far = pltpu.roll(far, a if way == 0 else 128 - a, 1)
                need = far > a
                t = free[way]
                if a > 0:
                    t = jnp.maximum(t, pltpu.roll(before[way], sgn, 1) + LAG)
                free[way] = jnp.where(need, t + PIECES, free[way])
                before[way] = jnp.where(need, t, -4096)
                starts[way, g * HOPS + a] = before[way]
        ends.append(jnp.max(jnp.maximum(free[0], free[1]), axis=1, keepdims=True))
    late = jnp.maximum(ends[0] - MID, ends[1] - STEPS)
    late = jnp.broadcast_to(late, shape)
    key = late * PLANS + lax.broadcasted_iota(jnp.int32, shape, 0)
    best = jnp.min(key, axis=0, keepdims=True)
    picked = key == best
    fits = jnp.where(best < PLANS, 1, 0)

    items = 2 * HOPS
    lane1 = lax.broadcasted_iota(jnp.int32, (1, 128), 1)
    sent, came = [], []
    for way in range(2):
        from_lane = lax.rem(z + members - 1, members) if way == 0 else lax.rem(z + 1, members)
        mine, theirs = [], []
        for r in range(items):
            row = jnp.sum(jnp.where(picked, starts[way, r], 0), axis=0, keepdims=True)
            mine.append(jnp.broadcast_to(jnp.sum(jnp.where(lane1 == z, row, 0), axis=1, keepdims=True), (1, 128)))
            theirs.append(
                jnp.broadcast_to(jnp.sum(jnp.where(lane1 == from_lane, row, 0), axis=1, keepdims=True), (1, 128))
            )
        sent.append(mine)
        came.append(theirs)
    top = 2 * PIECES + 2 * STEPS
    rows = []
    for way in range(2):
        base = 2 * PIECES + way * STEPS
        index = jnp.zeros((1, 128), jnp.int32)
        for g in range(2):
            for a in range(HOPS):
                at = sent[way][g * HOPS + a]
                first = g * PIECES if a == 0 else base + came[way][g * HOPS + a - 1]
                hit = (lane1 >= at) & (lane1 < at + PIECES)
                index = jnp.where(hit, first + lane1 - at, index)
        rows.append(jnp.clip(index, 0, top - 1))
    return rows, came, fits, lane1, top


def route_kernel(members, patches, *refs):
    (cb, ca, mask, e_in, f_in, g1, g2, wq_in, wk_in, wv_in, wo_in, wu_in, wd_in, out, fine) = refs[:15]
    scratch = list(refs[15:])
    nb = [scratch.pop(0) for _ in range(2)]
    wq, wk, wv, wo, wu, wd = [scratch.pop(0) for _ in range(6)]
    kb, vb, qb, mb, st, first, att, fx = [scratch.pop(0) for _ in range(8)]
    pool, staged, landed, starts, plan, table = [scratch.pop(0) for _ in range(6)]
    w_sem, own_sem, plan_sem, z_send, z_recv, h_send, h_recv = scratch

    z = lax.axis_index("member")
    p = lax.axis_index("patch")
    nodes, width = st.shape
    rows = nodes // PIECES

    def dz(off):
        return {"member": lax.rem(z + off + members, members)}

    def dp(off):
        return {"patch": lax.rem(p + off + patches, patches)}

    own = [
        pltpu.make_async_copy(src.at[0, pl.ds(c * rows, rows)], pool.at[g * PIECES + c], own_sem.at[g, c])
        for g, src in enumerate((e_in, f_in))
        for c in range(PIECES)
    ]
    for copy in own:
        copy.start()
    w_copies = [
        pltpu.make_async_copy(s, d, w_sem.at[i])
        for i, (s, d) in enumerate(zip((wq_in, wk_in, wv_in, wo_in, wu_in, wd_in), (wq, wk, wv, wo, wu, wd)))
    ]
    for w in w_copies:
        w.start()
    barrier = pltpu.get_barrier_semaphore()
    peers = [dz(1), dz(-1), dp(1), dp(-1), dp(2), dp(-2)]
    for peer in peers:
        pl.semaphore_signal(barrier, inc=1, device_id=peer, device_id_type=MESH)

    moved = [ca[s] for s in range(members)]
    sources = ([cb[m] for m in moved], moved)
    index, came, fits, lane1, top = make_plan(members, z, sources, starts, plan)
    mine = ca[z]
    finals = []
    for g, src in enumerate((cb[mine], mine)):
        dist = lax.rem(z - src + members, members)
        at = jnp.full((1, 128), g * PIECES, jnp.int32)
        for way in (1, 0):
            gone = dist if way == 0 else members - dist
            for a in range(HOPS):
                begin = came[way][g * HOPS + a]
                use = (begin >= 0) & (gone == a + 1)
                at = jnp.where(use, 2 * PIECES + way * STEPS + begin, at)
        finals.append(jnp.clip(at, 0, top - PIECES))
    plan[...] = jnp.zeros(plan.shape, jnp.int32)
    for r, row in enumerate((index[0], index[1], finals[0], finals[1], fits)):
        plan[pl.ds(r, 1)] = row
    to_smem = pltpu.make_async_copy(plan, table, plan_sem)
    to_smem.start()
    for copy in own:
        copy.wait()
    pl.semaphore_wait(barrier, len(peers))
    to_smem.wait()
    fine[0, 0] = table[4, 0]

    def hop(way, t):
        return pltpu.make_async_remote_copy(
            src_ref=staged.at[way, t],
            dst_ref=landed.at[way, t],
            send_sem=z_send.at[way],
            recv_sem=z_recv.at[way, t],
            device_id=dz(1 if way == 0 else -1),
            device_id_type=MESH,
        )

    def take(t):
        for way in range(2):
            hop(way, t).wait_recv()
            pool[2 * PIECES + way * STEPS + t] = landed[way, t]

    def give(t):
        for way in range(2):
            staged[way, t] = pool[table[way, t]]
            hop(way, t).start()

    def step(t):
        take(t - LAG)
        give(t)

    def piece(g, c):
        return pool[table[2 + g, 0] + c]

    publish, arrive, keys_values, queries, attend, finish, h_drain = drift_tools(
        PIECES, p, dp, mask, g1, g2, nb, wq, wk, wv, wo, wu, wd, kb, vb, qb, mb, att, h_send, h_recv
    )

    for t in range(LAG):
        give(t)

    @pl.loop(LAG, MID - PIECES + LAG)
    def _(t):
        step(t)

    for c in range(PIECES):
        step(MID - PIECES + LAG + c)
        x = piece(0, c)
        st[pl.ds(c * rows, rows)] = x
        publish(0, c, x)
    for w in w_copies:
        w.wait()
    now = MID + LAG
    queries(0)
    step(now)
    keys_values(0, 2)
    for t in range(now + 1, now + 6):
        step(t)
    now += 6
    for slot, count in ((1, 1), (3, 2), (0, 1), (4, 1)):
        arrive(0, slot)
        keys_values(0, slot)
        for t in range(now, now + count):
            step(t)
        now += count

    @pl.loop(0, HEADS)
    def _(h):
        attend(0, h)
        step(now + 2 * h)
        attend(1, h)
        step(now + 2 * h + 1)

    now += 2 * HEADS
    for t in range(now, STEPS):
        step(t)
    first[...] = finish(st)
    for c in range(PIECES):
        t = STEPS - PIECES + c
        if t >= STEPS - LAG:
            take(t)
        part = pl.ds(c * rows, rows)
        base = st[part].astype(F32) + 0.3 * piece(1, c).astype(F32)
        x = (base + 0.5 * first[part].astype(F32)).astype(BF)
        fx[part] = x
        publish(1, c, x)
    queries(1)
    keys_values(1, 2)
    for slot in (1, 3, 0, 4):
        arrive(1, slot)
        keys_values(1, slot)

    @pl.loop(0, HEADS)
    def _(h):
        attend(0, h)
        attend(1, h)

    second = finish(fx).astype(F32)
    for c in range(PIECES):
        part = pl.ds(c * rows, rows)
        base = st[part].astype(F32)
        tot = first[part].astype(F32) + second[c * rows : (c + 1) * rows]
        out[0, part] = (base + 0.25 * tot + 0.3 * piece(1, c).astype(F32)).astype(BF)

    h_drain()
    for way in range(2):
        pltpu.make_async_remote_copy(
            src_ref=staged.at[way],
            dst_ref=landed.at[way],
            send_sem=z_send.at[way],
            recv_sem=z_recv.at[way, 0],
            device_id=dz(1 if way == 0 else -1),
            device_id_type=MESH,
        ).wait_send()


def solution(mesh):
    members, patches = mesh.shape["member"], mesh.shape["patch"]

    def shards(ensemble, forcing, cb, ca, mask, g1, wq, wk, wv, wo, g2, wu, wd):
        _, nodes, width = ensemble.shape
        hidden = wu.shape[1]
        rows = nodes // CHUNKS
        head = width // HEADS
        smem = pl.BlockSpec(memory_space=pltpu.SMEM)
        vmem = pl.BlockSpec(memory_space=pltpu.VMEM)
        anym = pl.BlockSpec(memory_space=pl.ANY)
        state = jax.ShapeDtypeStruct(ensemble.shape, BF)
        common = (
            [pltpu.VMEM((5, nodes, width), BF) for _ in range(2)]
            + [pltpu.VMEM((width, width), BF) for _ in range(4)]
            + [pltpu.VMEM((width, hidden), BF), pltpu.VMEM((hidden, width), BF)]
            + [pltpu.VMEM((HEADS, 5 * nodes, head), BF) for _ in range(2)]
            + [pltpu.VMEM((HEADS, nodes, head), BF)]
            + [pltpu.VMEM((nodes, width), BF) for _ in range(3)]
            + [pltpu.VMEM((nodes, width), F32), pltpu.VMEM((nodes, width), BF)]
        )
        dma = pltpu.SemaphoreType.DMA

        def params(cid):
            return pltpu.CompilerParams(
                collective_id=cid, has_side_effects=True, vmem_limit_bytes=56 * 1024 * 1024
            )

        ins = [smem] * 3 + [anym] * 2 + [vmem] * 2 + [anym] * 6
        args = (cb, ca, mask, ensemble, forcing, g1.reshape(1, width), g2.reshape(1, width), wq, wk, wv, wo, wu, wd)
        size = nodes // PIECES
        out, fine = pl.pallas_call(
            functools.partial(route_kernel, members, patches),
            out_shape=(state, jax.ShapeDtypeStruct((1, 1), jnp.int32)),
            in_specs=ins,
            out_specs=(vmem, smem),
            scratch_shapes=common
            + [
                pltpu.VMEM((2 * PIECES + 2 * STEPS, size, width), BF),
                pltpu.VMEM((2, STEPS, size, width), BF),
                pltpu.VMEM((2, STEPS, size, width), BF),
                pltpu.VMEM((2, 2 * HOPS, PLANS, 128), jnp.int32),
                pltpu.VMEM((8, 128), jnp.int32),
                pltpu.SMEM((8, 128), jnp.int32),
                dma((6,)),
                dma((2, PIECES)),
                dma,
                dma((2,)),
                dma((2, STEPS)),
                dma((2, 5, PIECES)),
                dma((2, 5, PIECES)),
            ],
            compiler_params=params(0),
            name="route",
        )(*args)

        def slow(_):
            return pl.pallas_call(
                functools.partial(ring_kernel, members, patches),
                out_shape=state,
                in_specs=ins,
                out_specs=vmem,
                scratch_shapes=[pltpu.VMEM((members, rows, width), BF) for _ in range(2 * CHUNKS)]
                + common
                + [
                    dma((6,)),
                    dma((2, CHUNKS)),
                    dma((2, CHUNKS, 2)),
                    dma((2, CHUNKS, 2, members // 2)),
                    dma((2, 5, CHUNKS)),
                    dma((2, 5, CHUNKS)),
                ],
                compiler_params=params(1),
                name="ring",
            )(*args)

        return lax.cond(fine[0, 0] > 0, lambda x: x, slow, out)

    placed = (P("member", "patch", None),) * 2 + (P(), P(), P("patch", None)) + (P(),) * 8
    return jax.shard_map(
        shards, mesh=mesh, in_specs=placed, out_specs=P("member", "patch", None), check_vma=False
    )
```

```python
import functools

import jax
import jax.numpy as jnp
from jax import lax
from jax.experimental import pallas as pl
from jax.experimental.pallas import tpu as pltpu
from jax.sharding import PartitionSpec as P

HEADS = 4
BLOCK = 128
REACH = 4
CHUNKS = 4
PIECES = 8
LAG = 5
HOPS = 10
PLANS = 64
MID = 55
STEPS = 73
BEHIND = 3
MESH = pl.DeviceIdType.MESH
BF = jnp.bfloat16
F32 = jnp.float32


def dot(a, b):
    return jnp.dot(a, b, preferred_element_type=F32)


def dot_nt(a, b):
    return lax.dot_general(a, b, (((1,), (1,)), ((), ())), preferred_element_type=F32)


def rms(x, gain):
    scale = lax.rsqrt(jnp.mean(x * x, axis=-1, keepdims=True) + 1e-06)
    return (x * scale * gain).astype(BF)


def gelu(x):
    return 0.5 * x * (1.0 + jnp.tanh(0.7978845608028654 * (x + 0.044715 * x * x * x)))


def drift_tools(
    chunks, p, dp, mask, g1, g2, nb, wq, wk, wv, wo, wu, wd, kb, vb, qb, mb, att, h_send, h_recv
):
    _, nodes, width = nb[0].shape
    rows = nodes // chunks
    head = width // HEADS

    def halo(k, off, c):
        part = pl.ds(c * rows, rows)
        return pltpu.make_async_remote_copy(
            src_ref=nb[k].at[2, part],
            dst_ref=nb[k].at[2 - off, part],
            send_sem=h_send.at[k, 2 - off, c],
            recv_sem=h_recv.at[k, 2 - off, c],
            device_id=dp(off),
            device_id_type=MESH,
        )

    offsets = (1, -1, 2, -2)

    def publish(k, c, x):
        part = pl.ds(c * rows, rows)
        nb[k][2, part] = rms(x.astype(F32), g1[...])
        for off in offsets:
            halo(k, off, c).start()

    def arrive(k, slot):
        for c in range(chunks):
            halo(k, 2 - slot, c).wait_recv()

    def keys_values(k, slot):
        part = pl.ds(slot * nodes, nodes)
        src = nb[k][slot]
        ks = dot(src, wk[...]).astype(BF)
        vs = dot(src, wv[...]).astype(BF)
        for h in range(HEADS):
            kb[h, part] = ks[:, h * head : (h + 1) * head]
            vb[h, part] = vs[:, h * head : (h + 1) * head]

    def queries(k):
        qs = dot(nb[k][2], wq[...]).astype(BF)
        for h in range(HEADS):
            qb[h] = qs[:, h * head : (h + 1) * head]

    factor = 1.4426950408889634 / head**0.5
    span = 2 * REACH + 1

    def attend(b, h):
        kv = pl.ds(b * BLOCK, span * BLOCK)
        s = dot_nt(qb[h, pl.ds(b * BLOCK, BLOCK)], kb[h, kv]) * factor
        parts = []
        for i in range(span):
            piece = s[:, i * BLOCK : (i + 1) * BLOCK]
            if i != REACH:
                link = mask[b, i if i < REACH else i - 1]
                piece = piece + jnp.where(link > 0, F32(0.0), F32(-jnp.inf))
            parts.append(piece)
        s = jnp.concatenate(parts, axis=1)
        top = jnp.max(s, axis=1, keepdims=True)
        e = jnp.exp2(s - top)
        total = jnp.sum(e, axis=1, keepdims=True)
        mixed = dot(e.astype(BF), vb[h, kv]) / total
        mb[pl.ds(b * BLOCK, BLOCK), pl.ds(pl.multiple_of(h * head, head), head)] = mixed.astype(BF)

    def finish(state):
        att[...] = dot(mb[...], wo[...])
        lifted = state[...].astype(F32) + att[...]
        hidden = gelu(dot(rms(lifted, g2[...]), wu[...])).astype(BF)
        return (att[...] + dot(hidden, wd[...])).astype(BF)

    def h_drain():
        for k in range(2):
            for off in offsets:
                for c in range(chunks):
                    halo(k, off, c).wait_send()

    return publish, arrive, keys_values, queries, attend, finish, h_drain


def ring_kernel(members, patches, *refs):
    (cb, ca, mask, e_in, f_in, g1, g2, wq_in, wk_in, wv_in, wo_in, wu_in, wd_in, out) = refs[:14]
    scratch = list(refs[14:])
    zb = [[scratch.pop(0) for _ in range(CHUNKS)] for _ in range(2)]
    nb = [scratch.pop(0) for _ in range(2)]
    wq, wk, wv, wo, wu, wd = [scratch.pop(0) for _ in range(6)]
    kb, vb, qb, mb, st, first, att, fx = [scratch.pop(0) for _ in range(8)]
    w_sem, own_sem, z_send, z_recv, h_send, h_recv = scratch

    z = lax.axis_index("member")
    p = lax.axis_index("patch")
    nodes, width = st.shape
    rows = nodes // CHUNKS
    head = width // HEADS
    right_ages = members // 2
    left_ages = members - 1 - right_ages

    def dz(off):
        return {"member": lax.rem(z + off + members, members)}

    def dp(off):
        return {"patch": lax.rem(p + off + patches, patches)}

    w_copies = [
        pltpu.make_async_copy(s, d, w_sem.at[i])
        for i, (s, d) in enumerate(zip((wq_in, wk_in, wv_in, wo_in, wu_in, wd_in), (wq, wk, wv, wo, wu, wd)))
    ]
    own = [
        [
            pltpu.make_async_copy(src.at[0, pl.ds(c * rows, rows)], zb[g][c].at[0], own_sem.at[g, c])
            for c in range(CHUNKS)
        ]
        for g, src in enumerate((e_in, f_in))
    ]
    for g in range(2):
        for c in range(CHUNKS):
            own[g][c].start()
    for w in w_copies:
        w.start()

    barrier = pltpu.get_barrier_semaphore()
    peers = [dz(1), dz(-1), dp(1), dp(-1), dp(2), dp(-2)]
    for peer in peers:
        pl.semaphore_signal(barrier, inc=1, device_id=peer, device_id_type=MESH)
    pl.semaphore_wait(barrier, len(peers))

    def ring(g, c, way, age):
        if way == 0:
            src, dst = age, age + 1
        else:
            src, dst = lax.rem(members - age, members), members - 1 - age
        return pltpu.make_async_remote_copy(
            src_ref=zb[g][c].at[src],
            dst_ref=zb[g][c].at[dst],
            send_sem=z_send.at[g, c, way],
            recv_sem=z_recv.at[g, c, way, age],
            device_id=dz(1 if way == 0 else -1),
            device_id_type=MESH,
        )

    def z_first(g):
        for c in range(CHUNKS):
            own[g][c].wait()
            ring(g, c, 0, 0).start()
            ring(g, c, 1, 0).start()

    def z_step(g, age, chunks):
        for c in chunks:
            ring(g, c, 0, age - 1).wait_recv()
            ring(g, c, 0, age).start()
            ring(g, c, 1, age - 1).wait_recv()
            ring(g, c, 1, age).start()

    def z_last(g, chunks):
        for c in chunks:
            ring(g, c, 0, right_ages - 2).wait_recv()
            ring(g, c, 0, right_ages - 1).start()
            ring(g, c, 1, left_ages - 1).wait_recv()

    def z_end(g, c):
        ring(g, c, 0, right_ages - 1).wait_recv()

    def z_drain():
        for g in range(2):
            for c in range(CHUNKS):
                for way, ages in ((0, right_ages), (1, left_ages)):
                    part = zb[g][c].at[pl.ds(0, ages)]
                    pltpu.make_async_remote_copy(
                        src_ref=part,
                        dst_ref=part,
                        send_sem=z_send.at[g, c, way],
                        recv_sem=z_recv.at[g, c, way, 0],
                        device_id=dz(1 if way == 0 else -1),
                        device_id_type=MESH,
                    ).wait_send()

    publish, arrive, keys_values, queries, attend, finish, h_drain = drift_tools(
        CHUNKS, p, dp, mask, g1, g2, nb, wq, wk, wv, wo, wu, wd, kb, vb, qb, mb, att, h_send, h_recv
    )

    z_first(0)

    @pl.loop(1, left_ages)
    def _(age):
        z_step(0, age, range(CHUNKS))

    z_last(0, range(CHUNKS))
    z_first(1)

    d_e = lax.rem(z - cb[ca[z]] + members, members)
    d_f = lax.rem(z - ca[z] + members, members)
    for c in range(CHUNKS):
        z_end(0, c)
        part = pl.ds(c * rows, rows)
        x = zb[0][c][d_e]
        st[part] = x
        publish(0, c, x)
    for w in w_copies:
        w.wait()
    queries(0)
    keys_values(0, 2)
    z_step(1, 1, range(CHUNKS))
    for slot in (1, 3):
        arrive(0, slot)
        keys_values(0, slot)
    z_step(1, 2, range(CHUNKS))
    for slot in (0, 4):
        arrive(0, slot)
        keys_values(0, slot)

    half = CHUNKS // 2

    @pl.loop(0, HEADS)
    def _(h):
        attend(0, h)

        @pl.when(h < HEADS - 1)
        def _():
            z_step(1, 3 + h, range(half))

        attend(1, h)

        @pl.when(h < HEADS - 1)
        def _():
            z_step(1, 3 + h, range(half, CHUNKS))

    first[...] = finish(st)

    @pl.loop(3 + HEADS - 1, left_ages)
    def _(age):
        z_step(1, age, range(CHUNKS))

    z_last(1, range(CHUNKS))
    for c in range(CHUNKS):
        z_end(1, c)
        part = pl.ds(c * rows, rows)
        base = st[part].astype(F32) + 0.3 * zb[1][c][d_f].astype(F32)
        x = (base + 0.5 * first[part].astype(F32)).astype(BF)
        fx[part] = x
        publish(1, c, x)
    queries(1)
    keys_values(1, 2)
    for slot in (1, 3, 0, 4):
        arrive(1, slot)
        keys_values(1, slot)

    @pl.loop(0, HEADS)
    def _(h):
        attend(0, h)
        attend(1, h)

    second = finish(fx).astype(F32)
    for c in range(CHUNKS):
        part = pl.ds(c * rows, rows)
        base = st[part].astype(F32)
        tot = first[part].astype(F32) + second[c * rows : (c + 1) * rows]
        out[0, part] = (base + 0.25 * tot + 0.3 * zb[1][c][d_f].astype(F32)).astype(BF)

    h_drain()
    z_drain()


def thresholds(shape, members, g):
    q = lax.broadcasted_iota(jnp.int32, shape, 0)
    s = lax.rem(lax.broadcasted_iota(jnp.int32, shape, 1), members)
    x = (q * 40503 + s * 30011 + (g * 12289 + 7)) & 0xFFFF
    x = (x * 25173 + 13849) & 0xFFFF
    x = x ^ (x >> 7)
    x = (x * 25173 + 13849) & 0xFFFF
    x = x ^ (x >> 9)
    half = members // 2
    low = members - HOPS
    wide = low + ((x * (HOPS - low + 1)) >> 16)
    near = half - 1 + ((x * 2) >> 16)
    return jnp.where(q == 0, half, jnp.where(q == 1, half - 1, jnp.where(q < shape[0] // 4, near, wide)))


def make_plan(members, z, sources, starts, plan):
    shape = starts.shape[2:]
    lane = lax.broadcasted_iota(jnp.int32, shape, 1)
    slot = lax.rem(lane, members)
    zero = jnp.zeros(shape, jnp.int32)
    reach = []
    for g in range(2):
        src = zero
        for m in range(members):
            src = jnp.where(slot == m, sources[g][m], src)
        dist = lax.rem(slot - src + members, members)
        right = dist <= thresholds(shape, members, g)
        away = (jnp.where(right, dist, 0), jnp.where(right, 0, members - dist))
        both = []
        for way in range(2):
            far = zero
            for b in range(1, HOPS + 1):
                shift = (128 - b) if way == 0 else b
                far = jnp.where(pltpu.roll(away[way], shift, 1) == b, b, far)
            both.append(far)
        reach.append(both)
    free = [zero, zero]
    ends = [zero, zero]
    before = [[None, None], [None, None]]
    for g, a in sorted(((g, a) for g in range(2) for a in range(HOPS)), key=lambda hop: (hop[1] + BEHIND * hop[0], hop[0])):
        for way in range(2):
            sgn = 1 if way == 0 else 127
            far = reach[g][way]
            if a > 0:
                far = pltpu.roll(far, a if way == 0 else 128 - a, 1)
            need = far > a
            t = free[way]
            if a > 0:
                t = jnp.maximum(t, pltpu.roll(before[g][way], sgn, 1) + LAG)
            free[way] = jnp.where(need, t + PIECES, free[way])
            ends[g] = jnp.maximum(ends[g], jnp.where(need, t + PIECES, 0))
            before[g][way] = jnp.where(need, t, -4096)
            starts[way, g * HOPS + a] = before[g][way]
    ends = [jnp.max(end, axis=1, keepdims=True) for end in ends]
    late = jnp.maximum(ends[0] - MID, ends[1] - STEPS)
    late = jnp.broadcast_to(late, shape)
    key = late * PLANS + lax.broadcasted_iota(jnp.int32, shape, 0)
    best = jnp.min(key, axis=0, keepdims=True)
    picked = key == best
    fits = jnp.where(best < PLANS, 1, 0)

    items = 2 * HOPS
    lane1 = lax.broadcasted_iota(jnp.int32, (1, 128), 1)
    sent, came = [], []
    for way in range(2):
        from_lane = lax.rem(z + members - 1, members) if way == 0 else lax.rem(z + 1, members)
        mine, theirs = [], []
        for r in range(items):
            row = jnp.sum(jnp.where(picked, starts[way, r], 0), axis=0, keepdims=True)
            mine.append(jnp.broadcast_to(jnp.sum(jnp.where(lane1 == z, row, 0), axis=1, keepdims=True), (1, 128)))
            theirs.append(
                jnp.broadcast_to(jnp.sum(jnp.where(lane1 == from_lane, row, 0), axis=1, keepdims=True), (1, 128))
            )
        sent.append(mine)
        came.append(theirs)
    top = 2 * PIECES + 2 * STEPS
    rows = []
    for way in range(2):
        base = 2 * PIECES + way * STEPS
        index = jnp.zeros((1, 128), jnp.int32)
        for g in range(2):
            for a in range(HOPS):
                at = sent[way][g * HOPS + a]
                first = g * PIECES if a == 0 else base + came[way][g * HOPS + a - 1]
                hit = (lane1 >= at) & (lane1 < at + PIECES)
                index = jnp.where(hit, first + lane1 - at, index)
        rows.append(jnp.clip(index, 0, top - 1))
    return rows, came, fits, lane1, top


def route_kernel(members, patches, *refs):
    (cb, ca, mask, e_in, f_in, g1, g2, wq_in, wk_in, wv_in, wo_in, wu_in, wd_in, out, fine) = refs[:15]
    scratch = list(refs[15:])
    nb = [scratch.pop(0) for _ in range(2)]
    wq, wk, wv, wo, wu, wd = [scratch.pop(0) for _ in range(6)]
    kb, vb, qb, mb, st, first, att, fx = [scratch.pop(0) for _ in range(8)]
    pool, staged, landed, starts, plan, table = [scratch.pop(0) for _ in range(6)]
    w_sem, own_sem, plan_sem, z_send, z_recv, h_send, h_recv = scratch

    z = lax.axis_index("member")
    p = lax.axis_index("patch")
    nodes, width = st.shape
    rows = nodes // PIECES

    def dz(off):
        return {"member": lax.rem(z + off + members, members)}

    def dp(off):
        return {"patch": lax.rem(p + off + patches, patches)}

    own = [
        pltpu.make_async_copy(src.at[0, pl.ds(c * rows, rows)], pool.at[g * PIECES + c], own_sem.at[g, c])
        for g, src in enumerate((e_in, f_in))
        for c in range(PIECES)
    ]
    for copy in own:
        copy.start()
    w_copies = [
        pltpu.make_async_copy(s, d, w_sem.at[i])
        for i, (s, d) in enumerate(zip((wq_in, wk_in, wv_in, wo_in, wu_in, wd_in), (wq, wk, wv, wo, wu, wd)))
    ]
    for w in w_copies:
        w.start()
    barrier = pltpu.get_barrier_semaphore()
    peers = [dz(1), dz(-1), dp(1), dp(-1), dp(2), dp(-2)]
    for peer in peers:
        pl.semaphore_signal(barrier, inc=1, device_id=peer, device_id_type=MESH)

    moved = [ca[s] for s in range(members)]
    sources = ([cb[m] for m in moved], moved)
    index, came, fits, lane1, top = make_plan(members, z, sources, starts, plan)
    mine = ca[z]
    finals = []
    for g, src in enumerate((cb[mine], mine)):
        dist = lax.rem(z - src + members, members)
        at = jnp.full((1, 128), g * PIECES, jnp.int32)
        for way in (1, 0):
            gone = dist if way == 0 else members - dist
            for a in range(HOPS):
                begin = came[way][g * HOPS + a]
                use = (begin >= 0) & (gone == a + 1)
                at = jnp.where(use, 2 * PIECES + way * STEPS + begin, at)
        finals.append(jnp.clip(at, 0, top - PIECES))
    plan[...] = jnp.zeros(plan.shape, jnp.int32)
    for r, row in enumerate((index[0], index[1], finals[0], finals[1], fits)):
        plan[pl.ds(r, 1)] = row
    to_smem = pltpu.make_async_copy(plan, table, plan_sem)
    to_smem.start()
    for copy in own:
        copy.wait()
    pl.semaphore_wait(barrier, len(peers))
    to_smem.wait()
    fine[0, 0] = table[4, 0]

    def hop(way, t):
        return pltpu.make_async_remote_copy(
            src_ref=staged.at[way, t],
            dst_ref=landed.at[way, t],
            send_sem=z_send.at[way],
            recv_sem=z_recv.at[way, t],
            device_id=dz(1 if way == 0 else -1),
            device_id_type=MESH,
        )

    def take(t, way):
        hop(way, t).wait_recv()
        pool[2 * PIECES + way * STEPS + t] = landed[way, t]

    def give(t, way):
        staged[way, t] = pool[table[way, t]]
        hop(way, t).start()

    def step(t):
        for way in range(2):
            take(t - LAG, way)
            give(t, way)

    def piece(g, c):
        return pool[table[2 + g, 0] + c]

    publish, arrive, keys_values, queries, attend, finish, h_drain = drift_tools(
        PIECES, p, dp, mask, g1, g2, nb, wq, wk, wv, wo, wu, wd, kb, vb, qb, mb, att, h_send, h_recv
    )

    for t in range(LAG):
        for way in range(2):
            give(t, way)

    @pl.loop(LAG, MID - PIECES + LAG)
    def _(t):
        step(t)

    for c in range(PIECES):
        step(MID - PIECES + LAG + c)
        x = piece(0, c)
        st[pl.ds(c * rows, rows)] = x
        publish(0, c, x)
    for w in w_copies:
        w.wait()
    now = MID + LAG
    queries(0)
    step(now)
    keys_values(0, 2)
    for t in range(now + 1, now + 7):
        step(t)
    now += 7
    for slot, count in ((1, 1), (3, 1), (0, 2), (4, 2)):
        arrive(0, slot)
        keys_values(0, slot)
        for t in range(now, now + count):
            step(t)
        now += count
    for t in range(now, STEPS):
        step(t)

    @pl.loop(0, HEADS)
    def _(h):
        attend(0, h)
        attend(1, h)

    first[...] = finish(st)
    for c in range(PIECES):
        t = STEPS - PIECES + c
        if t >= STEPS - LAG:
            for way in range(2):
                take(t, way)
        part = pl.ds(c * rows, rows)
        base = st[part].astype(F32) + 0.3 * piece(1, c).astype(F32)
        x = (base + 0.5 * first[part].astype(F32)).astype(BF)
        fx[part] = x
        publish(1, c, x)
    queries(1)
    keys_values(1, 2)
    for slot in (1, 3, 0, 4):
        arrive(1, slot)
        keys_values(1, slot)

    @pl.loop(0, HEADS)
    def _(h):
        attend(0, h)
        attend(1, h)

    second = finish(fx).astype(F32)
    for c in range(PIECES):
        part = pl.ds(c * rows, rows)
        base = st[part].astype(F32)
        tot = first[part].astype(F32) + second[c * rows : (c + 1) * rows]
        out[0, part] = (base + 0.25 * tot + 0.3 * piece(1, c).astype(F32)).astype(BF)

    h_drain()
    for way in range(2):
        pltpu.make_async_remote_copy(
            src_ref=staged.at[way],
            dst_ref=landed.at[way],
            send_sem=z_send.at[way],
            recv_sem=z_recv.at[way, 0],
            device_id=dz(1 if way == 0 else -1),
            device_id_type=MESH,
        ).wait_send()


def solution(mesh):
    members, patches = mesh.shape["member"], mesh.shape["patch"]

    def shards(ensemble, forcing, cb, ca, mask, g1, wq, wk, wv, wo, g2, wu, wd):
        _, nodes, width = ensemble.shape
        hidden = wu.shape[1]
        rows = nodes // CHUNKS
        head = width // HEADS
        smem = pl.BlockSpec(memory_space=pltpu.SMEM)
        vmem = pl.BlockSpec(memory_space=pltpu.VMEM)
        anym = pl.BlockSpec(memory_space=pl.ANY)
        state = jax.ShapeDtypeStruct(ensemble.shape, BF)
        common = (
            [pltpu.VMEM((5, nodes, width), BF) for _ in range(2)]
            + [pltpu.VMEM((width, width), BF) for _ in range(4)]
            + [pltpu.VMEM((width, hidden), BF), pltpu.VMEM((hidden, width), BF)]
            + [pltpu.VMEM((HEADS, 5 * nodes, head), BF) for _ in range(2)]
            + [pltpu.VMEM((HEADS, nodes, head), BF)]
            + [pltpu.VMEM((nodes, width), BF) for _ in range(3)]
            + [pltpu.VMEM((nodes, width), F32), pltpu.VMEM((nodes, width), BF)]
        )
        dma = pltpu.SemaphoreType.DMA

        def params(cid):
            return pltpu.CompilerParams(
                collective_id=cid, has_side_effects=True, vmem_limit_bytes=56 * 1024 * 1024
            )

        ins = [smem] * 3 + [anym] * 2 + [vmem] * 2 + [anym] * 6
        args = (cb, ca, mask, ensemble, forcing, g1.reshape(1, width), g2.reshape(1, width), wq, wk, wv, wo, wu, wd)
        size = nodes // PIECES
        out, fine = pl.pallas_call(
            functools.partial(route_kernel, members, patches),
            out_shape=(state, jax.ShapeDtypeStruct((1, 1), jnp.int32)),
            in_specs=ins,
            out_specs=(vmem, smem),
            scratch_shapes=common
            + [
                pltpu.VMEM((2 * PIECES + 2 * STEPS, size, width), BF),
                pltpu.VMEM((2, STEPS, size, width), BF),
                pltpu.VMEM((2, STEPS, size, width), BF),
                pltpu.VMEM((2, 2 * HOPS, PLANS, 128), jnp.int32),
                pltpu.VMEM((8, 128), jnp.int32),
                pltpu.SMEM((8, 128), jnp.int32),
                dma((6,)),
                dma((2, PIECES)),
                dma,
                dma((2,)),
                dma((2, STEPS)),
                dma((2, 5, PIECES)),
                dma((2, 5, PIECES)),
            ],
            compiler_params=params(0),
            name="route",
        )(*args)

        def slow(_):
            return pl.pallas_call(
                functools.partial(ring_kernel, members, patches),
                out_shape=state,
                in_specs=ins,
                out_specs=vmem,
                scratch_shapes=[pltpu.VMEM((members, rows, width), BF) for _ in range(2 * CHUNKS)]
                + common
                + [
                    dma((6,)),
                    dma((2, CHUNKS)),
                    dma((2, CHUNKS, 2)),
                    dma((2, CHUNKS, 2, members // 2)),
                    dma((2, 5, CHUNKS)),
                    dma((2, 5, CHUNKS)),
                ],
                compiler_params=params(1),
                name="ring",
            )(*args)

        return lax.cond(fine[0, 0] > 0, lambda x: x, slow, out)

    placed = (P("member", "patch", None),) * 2 + (P(), P(), P("patch", None)) + (P(),) * 8
    return jax.shard_map(
        shards, mesh=mesh, in_specs=placed, out_specs=P("member", "patch", None), check_vma=False
    )
```

```python
import functools

import jax
import jax.numpy as jnp
from jax import lax
from jax.experimental import pallas as pl
from jax.experimental.pallas import tpu as pltpu
from jax.sharding import PartitionSpec as P

HEADS = 4
BLOCK = 128
REACH = 4
CHUNKS = 4
PIECES = 8
LAG = 5
HOPS = 10
PLANS = 64
MID = 55
STEPS = 73
BEHIND = 3
MESH = pl.DeviceIdType.MESH
BF = jnp.bfloat16
F32 = jnp.float32


def dot(a, b):
    return jnp.dot(a, b, preferred_element_type=F32)


def dot_nt(a, b):
    return lax.dot_general(a, b, (((1,), (1,)), ((), ())), preferred_element_type=F32)


def rms(x, gain):
    scale = lax.rsqrt(jnp.mean(x * x, axis=-1, keepdims=True) + 1e-06)
    return (x * scale * gain).astype(BF)


def gelu(x):
    return 0.5 * x * (1.0 + jnp.tanh(0.7978845608028654 * (x + 0.044715 * x * x * x)))


def drift_tools(
    chunks, p, dp, mask, g1, g2, nb, wq, wk, wv, wo, wu, wd, kb, vb, qb, mb, att, h_send, h_recv
):
    _, nodes, width = nb[0].shape
    rows = nodes // chunks
    head = width // HEADS

    side = 2 * lax.rem(p, 2) - 1
    partner, outer, same, last = 2 - side, 2 + side, 2 + 2 * side, 2 - 2 * side

    def copy_rows(k, c, src, dst, off, sem):
        part = pl.ds(c * rows, rows)
        return pltpu.make_async_remote_copy(
            src_ref=nb[k].at[src, part],
            dst_ref=nb[k].at[dst, part],
            send_sem=h_send.at[k, sem, c],
            recv_sem=h_recv.at[k, dst, c],
            device_id=dp(off),
            device_id_type=MESH,
        )

    def sends(k, c):
        return (
            copy_rows(k, c, 2, partner, side, 1),
            copy_rows(k, c, 2, same, -2 * side, 2),
            copy_rows(k, c, 2, outer, -side, 0),
        )

    def hand_on(k, c):
        return copy_rows(k, c, outer, same, -side, 3)

    def publish(k, c, x):
        part = pl.ds(c * rows, rows)
        nb[k][2, part] = rms(x.astype(F32), g1[...])
        for send in sends(k, c):
            send.start()

    def relay(k, c):
        copy_rows(k, c, 2, outer, side, 0).wait_recv()
        hand_on(k, c).start()

    def arrive(k, slot):
        for c in range(chunks):
            copy_rows(k, c, 2, slot, side, 0).wait_recv()

    def keys_values(k, slot):
        part = pl.ds(pl.multiple_of(slot * nodes, nodes), nodes)
        src = nb[k][slot]
        ks = dot(src, wk[...]).astype(BF)
        vs = dot(src, wv[...]).astype(BF)
        for h in range(HEADS):
            kb[h, part] = ks[:, h * head : (h + 1) * head]
            vb[h, part, pl.ds(0, head)] = vs[:, h * head : (h + 1) * head]

    def queries(k):
        qs = dot(nb[k][2], wq[...]).astype(BF)
        for h in range(HEADS):
            qb[h] = qs[:, h * head : (h + 1) * head]

    factor = 1.4426950408889634 / head**0.5
    span = 2 * REACH + 1

    def attend(b, h):
        kv = pl.ds(b * BLOCK, span * BLOCK)
        s = dot_nt(qb[h, pl.ds(b * BLOCK, BLOCK)], kb[h, kv]) * factor
        parts = []
        for i in range(span):
            piece = s[:, i * BLOCK : (i + 1) * BLOCK]
            if i != REACH:
                link = mask[b, i if i < REACH else i - 1]
                piece = piece + jnp.where(link > 0, F32(0.0), F32(-jnp.inf))
            parts.append(piece)
        s = jnp.concatenate(parts, axis=1)
        top = jnp.max(s, axis=1, keepdims=True)
        e = jnp.exp2(s - top)
        total = jnp.sum(e, axis=1, keepdims=True)
        mixed = dot(e.astype(BF), vb[h, kv, pl.ds(0, head)]) / total
        mb[pl.ds(b * BLOCK, BLOCK), pl.ds(pl.multiple_of(h * head, head), head)] = mixed.astype(BF)

    def attend_all(h):
        s = dot_nt(qb[h], kb[h]) * factor
        probs = []
        for b in range(nodes // BLOCK):
            parts = []
            for i in range(span):
                piece = s[b * BLOCK : (b + 1) * BLOCK, (b + i) * BLOCK : (b + i + 1) * BLOCK]
                if i != REACH:
                    link = mask[b, i if i < REACH else i - 1]
                    piece = piece + jnp.where(link > 0, F32(0.0), F32(-jnp.inf))
                parts.append(piece)
            sb = jnp.concatenate(parts, axis=1)
            e = jnp.exp2(sb - jnp.max(sb, axis=1, keepdims=True)).astype(BF)
            blank = jnp.zeros((BLOCK, BLOCK), BF)
            probs.append(jnp.concatenate([blank] * b + [e] + [blank] * (nodes // BLOCK - 1 - b), axis=1))
        both = dot(jnp.concatenate(probs, axis=0), vb[h])
        mixed = both[:, :head] / both[:, head:]
        mb[:, pl.ds(pl.multiple_of(h * head, head), head)] = mixed.astype(BF)

    def finish(state):
        att[...] = dot(mb[...], wo[...])
        lifted = state[...].astype(F32) + att[...]
        hidden = gelu(dot(rms(lifted, g2[...]), wu[...])).astype(BF)
        return (att[...] + dot(hidden, wd[...])).astype(BF)

    def h_drain():
        for k in range(2):
            for c in range(chunks):
                for send in sends(k, c) + (hand_on(k, c),):
                    send.wait_send()

    return (partner, outer, same, last), publish, relay, arrive, keys_values, queries, attend, attend_all, finish, h_drain


def ring_kernel(members, patches, *refs):
    (cb, ca, mask, e_in, f_in, g1, g2, wq_in, wk_in, wv_in, wo_in, wu_in, wd_in, out) = refs[:14]
    scratch = list(refs[14:])
    zb = [[scratch.pop(0) for _ in range(CHUNKS)] for _ in range(2)]
    nb = [scratch.pop(0) for _ in range(2)]
    wq, wk, wv, wo, wu, wd = [scratch.pop(0) for _ in range(6)]
    kb, vb, qb, mb, st, first, att, fx = [scratch.pop(0) for _ in range(8)]
    w_sem, own_sem, z_send, z_recv, h_send, h_recv = scratch

    z = lax.axis_index("member")
    p = lax.axis_index("patch")
    nodes, width = st.shape
    rows = nodes // CHUNKS
    head = width // HEADS
    right_ages = members // 2
    left_ages = members - 1 - right_ages

    def dz(off):
        return {"member": lax.rem(z + off + members, members)}

    def dp(off):
        return {"patch": lax.rem(p + off + patches, patches)}

    w_copies = [
        pltpu.make_async_copy(s, d, w_sem.at[i])
        for i, (s, d) in enumerate(zip((wq_in, wk_in, wv_in, wo_in, wu_in, wd_in), (wq, wk, wv, wo, wu, wd)))
    ]
    own = [
        [
            pltpu.make_async_copy(src.at[0, pl.ds(c * rows, rows)], zb[g][c].at[0], own_sem.at[g, c])
            for c in range(CHUNKS)
        ]
        for g, src in enumerate((e_in, f_in))
    ]
    for g in range(2):
        for c in range(CHUNKS):
            own[g][c].start()
    for w in w_copies:
        w.start()

    barrier = pltpu.get_barrier_semaphore()
    peers = [dz(1), dz(-1), dp(1), dp(-1), dp(2), dp(-2)]
    for peer in peers:
        pl.semaphore_signal(barrier, inc=1, device_id=peer, device_id_type=MESH)
    pl.semaphore_wait(barrier, len(peers))

    def ring(g, c, way, age):
        if way == 0:
            src, dst = age, age + 1
        else:
            src, dst = lax.rem(members - age, members), members - 1 - age
        return pltpu.make_async_remote_copy(
            src_ref=zb[g][c].at[src],
            dst_ref=zb[g][c].at[dst],
            send_sem=z_send.at[g, c, way],
            recv_sem=z_recv.at[g, c, way, age],
            device_id=dz(1 if way == 0 else -1),
            device_id_type=MESH,
        )

    def z_first(g):
        for c in range(CHUNKS):
            own[g][c].wait()
            ring(g, c, 0, 0).start()
            ring(g, c, 1, 0).start()

    def z_step(g, age, chunks):
        for c in chunks:
            ring(g, c, 0, age - 1).wait_recv()
            ring(g, c, 0, age).start()
            ring(g, c, 1, age - 1).wait_recv()
            ring(g, c, 1, age).start()

    def z_last(g, chunks):
        for c in chunks:
            ring(g, c, 0, right_ages - 2).wait_recv()
            ring(g, c, 0, right_ages - 1).start()
            ring(g, c, 1, left_ages - 1).wait_recv()

    def z_end(g, c):
        ring(g, c, 0, right_ages - 1).wait_recv()

    def z_drain():
        for g in range(2):
            for c in range(CHUNKS):
                for way, ages in ((0, right_ages), (1, left_ages)):
                    part = zb[g][c].at[pl.ds(0, ages)]
                    pltpu.make_async_remote_copy(
                        src_ref=part,
                        dst_ref=part,
                        send_sem=z_send.at[g, c, way],
                        recv_sem=z_recv.at[g, c, way, 0],
                        device_id=dz(1 if way == 0 else -1),
                        device_id_type=MESH,
                    ).wait_send()

    slots, publish, relay, arrive, keys_values, queries, attend, _, finish, h_drain = drift_tools(
        CHUNKS, p, dp, mask, g1, g2, nb, wq, wk, wv, wo, wu, wd, kb, vb, qb, mb, att, h_send, h_recv
    )

    z_first(0)

    @pl.loop(1, left_ages)
    def _(age):
        z_step(0, age, range(CHUNKS))

    z_last(0, range(CHUNKS))
    z_first(1)

    d_e = lax.rem(z - cb[ca[z]] + members, members)
    d_f = lax.rem(z - ca[z] + members, members)
    for c in range(CHUNKS):
        z_end(0, c)
        part = pl.ds(c * rows, rows)
        x = zb[0][c][d_e]
        st[part] = x
        publish(0, c, x)
    for w in w_copies:
        w.wait()
    queries(0)
    keys_values(0, 2)
    z_step(1, 1, range(CHUNKS))
    partner, outer, same, last = slots
    for c in range(CHUNKS):
        relay(0, c)
    arrive(0, partner)
    keys_values(0, partner)
    keys_values(0, outer)
    z_step(1, 2, range(CHUNKS))
    for slot in (same, last):
        arrive(0, slot)
        keys_values(0, slot)

    half = CHUNKS // 2

    @pl.loop(0, HEADS)
    def _(h):
        attend(0, h)

        @pl.when(h < HEADS - 1)
        def _():
            z_step(1, 3 + h, range(half))

        attend(1, h)

        @pl.when(h < HEADS - 1)
        def _():
            z_step(1, 3 + h, range(half, CHUNKS))

    first[...] = finish(st)

    @pl.loop(3 + HEADS - 1, left_ages)
    def _(age):
        z_step(1, age, range(CHUNKS))

    z_last(1, range(CHUNKS))
    for c in range(CHUNKS):
        z_end(1, c)
        part = pl.ds(c * rows, rows)
        base = st[part].astype(F32) + 0.3 * zb[1][c][d_f].astype(F32)
        x = (base + 0.5 * first[part].astype(F32)).astype(BF)
        fx[part] = x
        publish(1, c, x)
    queries(1)
    keys_values(1, 2)
    for c in range(CHUNKS):
        relay(1, c)
    arrive(1, partner)
    keys_values(1, partner)
    keys_values(1, outer)
    for slot in (same, last):
        arrive(1, slot)
        keys_values(1, slot)

    @pl.loop(0, HEADS)
    def _(h):
        attend(0, h)
        attend(1, h)

    second = finish(fx).astype(F32)
    for c in range(CHUNKS):
        part = pl.ds(c * rows, rows)
        base = st[part].astype(F32)
        tot = first[part].astype(F32) + second[c * rows : (c + 1) * rows]
        out[0, part] = (base + 0.25 * tot + 0.3 * zb[1][c][d_f].astype(F32)).astype(BF)

    h_drain()
    z_drain()


def thresholds(shape, members, g):
    q = lax.broadcasted_iota(jnp.int32, shape, 0)
    s = lax.rem(lax.broadcasted_iota(jnp.int32, shape, 1), members)
    x = (q * 40503 + s * 30011 + (g * 12289 + 7)) & 0xFFFF
    x = (x * 25173 + 13849) & 0xFFFF
    x = x ^ (x >> 7)
    x = (x * 25173 + 13849) & 0xFFFF
    x = x ^ (x >> 9)
    half = members // 2
    low = members - HOPS
    wide = low + ((x * (HOPS - low + 1)) >> 16)
    near = half - 1 + ((x * 2) >> 16)
    return jnp.where(q == 0, half, jnp.where(q == 1, half - 1, jnp.where(q < shape[0] // 4, near, wide)))


def make_plan(members, z, sources, starts, plan):
    shape = starts.shape[2:]
    lane = lax.broadcasted_iota(jnp.int32, shape, 1)
    slot = lax.rem(lane, members)
    zero = jnp.zeros(shape, jnp.int32)
    reach = []
    for g in range(2):
        src = zero
        for m in range(members):
            src = jnp.where(slot == m, sources[g][m], src)
        dist = lax.rem(slot - src + members, members)
        right = dist <= thresholds(shape, members, g)
        away = (jnp.where(right, dist, 0), jnp.where(right, 0, members - dist))
        both = []
        for way in range(2):
            far = zero
            for b in range(1, HOPS + 1):
                shift = (128 - b) if way == 0 else b
                far = jnp.where(pltpu.roll(away[way], shift, 1) == b, b, far)
            both.append(far)
        reach.append(both)
    free = [zero, zero]
    ends = [zero, zero]
    before = [[None, None], [None, None]]
    for g, a in sorted(((g, a) for g in range(2) for a in range(HOPS)), key=lambda hop: (hop[1] + BEHIND * hop[0], hop[0])):
        for way in range(2):
            sgn = 1 if way == 0 else 127
            far = reach[g][way]
            if a > 0:
                far = pltpu.roll(far, a if way == 0 else 128 - a, 1)
            need = far > a
            t = free[way]
            if a > 0:
                t = jnp.maximum(t, pltpu.roll(before[g][way], sgn, 1) + LAG)
            free[way] = jnp.where(need, t + PIECES, free[way])
            ends[g] = jnp.maximum(ends[g], jnp.where(need, t + PIECES, 0))
            before[g][way] = jnp.where(need, t, -4096)
            starts[way, g * HOPS + a] = before[g][way]
    ends = [jnp.max(end, axis=1, keepdims=True) for end in ends]
    late = jnp.maximum(ends[0] - MID, ends[1] - STEPS)
    late = jnp.broadcast_to(late, shape)
    key = late * PLANS + lax.broadcasted_iota(jnp.int32, shape, 0)
    best = jnp.min(key, axis=0, keepdims=True)
    picked = key == best
    fits = jnp.where(best < PLANS, 1, 0)

    items = 2 * HOPS
    lane1 = lax.broadcasted_iota(jnp.int32, (1, 128), 1)
    sent, came = [], []
    for way in range(2):
        from_lane = lax.rem(z + members - 1, members) if way == 0 else lax.rem(z + 1, members)
        mine, theirs = [], []
        for r in range(items):
            row = jnp.sum(jnp.where(picked, starts[way, r], 0), axis=0, keepdims=True)
            mine.append(jnp.broadcast_to(jnp.sum(jnp.where(lane1 == z, row, 0), axis=1, keepdims=True), (1, 128)))
            theirs.append(
                jnp.broadcast_to(jnp.sum(jnp.where(lane1 == from_lane, row, 0), axis=1, keepdims=True), (1, 128))
            )
        sent.append(mine)
        came.append(theirs)
    top = 2 * PIECES + 2 * STEPS
    rows = []
    for way in range(2):
        base = 2 * PIECES + way * STEPS
        index = jnp.zeros((1, 128), jnp.int32)
        for g in range(2):
            for a in range(HOPS):
                at = sent[way][g * HOPS + a]
                first = g * PIECES if a == 0 else base + came[way][g * HOPS + a - 1]
                hit = (lane1 >= at) & (lane1 < at + PIECES)
                index = jnp.where(hit, first + lane1 - at, index)
        rows.append(jnp.clip(index, 0, top - 1))
    return rows, came, fits, lane1, top


def route_kernel(members, patches, *refs):
    (cb, ca, mask, e_in, f_in, g1, g2, wq_in, wk_in, wv_in, wo_in, wu_in, wd_in, out, fine) = refs[:15]
    scratch = list(refs[15:])
    nb = [scratch.pop(0) for _ in range(2)]
    wq, wk, wv, wo, wu, wd = [scratch.pop(0) for _ in range(6)]
    kb, vb, qb, mb, st, first, att, fx = [scratch.pop(0) for _ in range(8)]
    pool, staged, landed, starts, plan, table = [scratch.pop(0) for _ in range(6)]
    w_sem, own_sem, plan_sem, z_send, z_recv, h_send, h_recv = scratch

    z = lax.axis_index("member")
    p = lax.axis_index("patch")
    nodes, width = st.shape
    rows = nodes // PIECES

    def dz(off):
        return {"member": lax.rem(z + off + members, members)}

    def dp(off):
        return {"patch": lax.rem(p + off + patches, patches)}

    own = [
        pltpu.make_async_copy(src.at[0, pl.ds(c * rows, rows)], pool.at[g * PIECES + c], own_sem.at[g, c])
        for g, src in enumerate((e_in, f_in))
        for c in range(PIECES)
    ]
    for copy in own:
        copy.start()
    w_copies = [
        pltpu.make_async_copy(s, d, w_sem.at[i])
        for i, (s, d) in enumerate(zip((wq_in, wk_in, wv_in, wo_in, wu_in, wd_in), (wq, wk, wv, wo, wu, wd)))
    ]
    for w in w_copies:
        w.start()
    barrier = pltpu.get_barrier_semaphore()
    peers = [dz(1), dz(-1), dp(1), dp(-1), dp(2), dp(-2)]
    for peer in peers:
        pl.semaphore_signal(barrier, inc=1, device_id=peer, device_id_type=MESH)

    moved = [ca[s] for s in range(members)]
    sources = ([cb[m] for m in moved], moved)
    index, came, fits, lane1, top = make_plan(members, z, sources, starts, plan)
    mine = ca[z]
    finals = []
    for g, src in enumerate((cb[mine], mine)):
        dist = lax.rem(z - src + members, members)
        at = jnp.full((1, 128), g * PIECES, jnp.int32)
        for way in (1, 0):
            gone = dist if way == 0 else members - dist
            for a in range(HOPS):
                begin = came[way][g * HOPS + a]
                use = (begin >= 0) & (gone == a + 1)
                at = jnp.where(use, 2 * PIECES + way * STEPS + begin, at)
        finals.append(jnp.clip(at, 0, top - PIECES))
    plan[...] = jnp.zeros(plan.shape, jnp.int32)
    for r, row in enumerate((index[0], index[1], finals[0], finals[1], fits)):
        plan[pl.ds(r, 1)] = row
    to_smem = pltpu.make_async_copy(plan, table, plan_sem)
    to_smem.start()
    for h in range(HEADS):
        vb[h, :, pl.ds(width // HEADS, width // HEADS)] = jnp.ones((vb.shape[1], width // HEADS), BF)
    for copy in own:
        copy.wait()
    pl.semaphore_wait(barrier, len(peers))
    to_smem.wait()
    fine[0, 0] = table[4, 0]

    def hop(way, t):
        return pltpu.make_async_remote_copy(
            src_ref=staged.at[way, t],
            dst_ref=landed.at[way, t],
            send_sem=z_send.at[way],
            recv_sem=z_recv.at[way, t],
            device_id=dz(1 if way == 0 else -1),
            device_id_type=MESH,
        )

    def take(t, way):
        hop(way, t).wait_recv()
        pool[2 * PIECES + way * STEPS + t] = landed[way, t]

    def give(t, way):
        staged[way, t] = pool[table[way, t]]
        hop(way, t).start()

    def step(t):
        for way in range(2):
            take(t - LAG, way)
            give(t, way)

    def piece(g, c):
        return pool[table[2 + g, 0] + c]

    slots, publish, relay, arrive, keys_values, queries, _, attend_all, finish, h_drain = drift_tools(
        PIECES, p, dp, mask, g1, g2, nb, wq, wk, wv, wo, wu, wd, kb, vb, qb, mb, att, h_send, h_recv
    )

    for t in range(LAG):
        for way in range(2):
            give(t, way)

    @pl.loop(LAG, MID - PIECES + LAG)
    def _(t):
        step(t)

    partner, outer, same, last = slots
    delay = 5
    for c in range(PIECES):
        step(MID - PIECES + LAG + c)
        x = piece(0, c)
        st[pl.ds(c * rows, rows)] = x
        publish(0, c, x)
        if c >= delay:
            relay(0, c - delay)
    for w in w_copies:
        w.wait()
    now = MID + LAG
    queries(0)
    step(now)
    relay(0, PIECES - delay)
    keys_values(0, 2)
    step(now + 1)
    relay(0, PIECES - delay + 1)
    arrive(0, partner)
    step(now + 2)
    relay(0, PIECES - delay + 2)
    keys_values(0, partner)
    step(now + 3)
    relay(0, PIECES - delay + 3)
    step(now + 4)
    relay(0, PIECES - delay + 4)
    keys_values(0, outer)
    now += 5
    for slot, count in ((same, 2), (last, 2)):
        arrive(0, slot)
        keys_values(0, slot)
        for t in range(now, now + count):
            step(t)
        now += count
    for t in range(now, STEPS):
        step(t)

    for h in range(HEADS):
        attend_all(h)

    first[...] = finish(st)
    for c in range(PIECES):
        t = STEPS - PIECES + c
        if t >= STEPS - LAG:
            for way in range(2):
                take(t, way)
        part = pl.ds(c * rows, rows)
        base = st[part].astype(F32) + 0.3 * piece(1, c).astype(F32)
        x = (base + 0.5 * first[part].astype(F32)).astype(BF)
        fx[part] = x
        publish(1, c, x)
    queries(1)
    keys_values(1, 2)
    for c in range(PIECES // 2):
        relay(1, c)
    arrive(1, partner)
    keys_values(1, partner)
    for c in range(PIECES // 2, PIECES):
        relay(1, c)
    keys_values(1, outer)
    for slot in (same, last):
        arrive(1, slot)
        keys_values(1, slot)

    for h in range(HEADS):
        attend_all(h)

    second = finish(fx).astype(F32)
    for c in range(PIECES):
        part = pl.ds(c * rows, rows)
        base = st[part].astype(F32)
        tot = first[part].astype(F32) + second[c * rows : (c + 1) * rows]
        out[0, part] = (base + 0.25 * tot + 0.3 * piece(1, c).astype(F32)).astype(BF)

    h_drain()
    for way in range(2):
        pltpu.make_async_remote_copy(
            src_ref=staged.at[way],
            dst_ref=landed.at[way],
            send_sem=z_send.at[way],
            recv_sem=z_recv.at[way, 0],
            device_id=dz(1 if way == 0 else -1),
            device_id_type=MESH,
        ).wait_send()


def solution(mesh):
    members, patches = mesh.shape["member"], mesh.shape["patch"]

    def shards(ensemble, forcing, cb, ca, mask, g1, wq, wk, wv, wo, g2, wu, wd):
        _, nodes, width = ensemble.shape
        hidden = wu.shape[1]
        rows = nodes // CHUNKS
        head = width // HEADS
        smem = pl.BlockSpec(memory_space=pltpu.SMEM)
        vmem = pl.BlockSpec(memory_space=pltpu.VMEM)
        anym = pl.BlockSpec(memory_space=pl.ANY)
        state = jax.ShapeDtypeStruct(ensemble.shape, BF)
        common = (
            [pltpu.VMEM((5, nodes, width), BF) for _ in range(2)]
            + [pltpu.VMEM((width, width), BF) for _ in range(4)]
            + [pltpu.VMEM((width, hidden), BF), pltpu.VMEM((hidden, width), BF)]
            + [pltpu.VMEM((HEADS, 5 * nodes, head), BF), pltpu.VMEM((HEADS, 5 * nodes, 2 * head), BF)]
            + [pltpu.VMEM((HEADS, nodes, head), BF)]
            + [pltpu.VMEM((nodes, width), BF) for _ in range(3)]
            + [pltpu.VMEM((nodes, width), F32), pltpu.VMEM((nodes, width), BF)]
        )
        dma = pltpu.SemaphoreType.DMA

        def params(cid):
            return pltpu.CompilerParams(
                collective_id=cid, has_side_effects=True, vmem_limit_bytes=56 * 1024 * 1024
            )

        ins = [smem] * 3 + [anym] * 2 + [vmem] * 2 + [anym] * 6
        args = (cb, ca, mask, ensemble, forcing, g1.reshape(1, width), g2.reshape(1, width), wq, wk, wv, wo, wu, wd)
        size = nodes // PIECES
        out, fine = pl.pallas_call(
            functools.partial(route_kernel, members, patches),
            out_shape=(state, jax.ShapeDtypeStruct((1, 1), jnp.int32)),
            in_specs=ins,
            out_specs=(vmem, smem),
            scratch_shapes=common
            + [
                pltpu.VMEM((2 * PIECES + 2 * STEPS, size, width), BF),
                pltpu.VMEM((2, STEPS, size, width), BF),
                pltpu.VMEM((2, STEPS, size, width), BF),
                pltpu.VMEM((2, 2 * HOPS, PLANS, 128), jnp.int32),
                pltpu.VMEM((8, 128), jnp.int32),
                pltpu.SMEM((8, 128), jnp.int32),
                dma((6,)),
                dma((2, PIECES)),
                dma,
                dma((2,)),
                dma((2, STEPS)),
                dma((2, 5, PIECES)),
                dma((2, 5, PIECES)),
            ],
            compiler_params=params(0),
            name="route",
        )(*args)

        def slow(_):
            return pl.pallas_call(
                functools.partial(ring_kernel, members, patches),
                out_shape=state,
                in_specs=ins,
                out_specs=vmem,
                scratch_shapes=[pltpu.VMEM((members, rows, width), BF) for _ in range(2 * CHUNKS)]
                + common
                + [
                    dma((6,)),
                    dma((2, CHUNKS)),
                    dma((2, CHUNKS, 2)),
                    dma((2, CHUNKS, 2, members // 2)),
                    dma((2, 5, CHUNKS)),
                    dma((2, 5, CHUNKS)),
                ],
                compiler_params=params(1),
                name="ring",
            )(*args)

        return lax.cond(fine[0, 0] > 0, lambda x: x, slow, out)

    placed = (P("member", "patch", None),) * 2 + (P(), P(), P("patch", None)) + (P(),) * 8
    return jax.shard_map(
        shards, mesh=mesh, in_specs=placed, out_specs=P("member", "patch", None), check_vma=False
    )
```

```python
import functools

import jax
import jax.numpy as jnp
from jax import lax
from jax.experimental import pallas as pl
from jax.experimental.pallas import tpu as pltpu
from jax.sharding import PartitionSpec as P

HEADS = 4
BLOCK = 128
REACH = 4
CHUNKS = 4
PIECES = 8
LAG = 5
HOPS = 10
PLANS = 64
MID = 55
STEPS = 73
BEHIND = 3
MESH = pl.DeviceIdType.MESH
BF = jnp.bfloat16
F32 = jnp.float32


def dot(a, b):
    return jnp.dot(a, b, preferred_element_type=F32)


def dot_nt(a, b):
    return lax.dot_general(a, b, (((1,), (1,)), ((), ())), preferred_element_type=F32)


def rms(x, gain):
    scale = lax.rsqrt(jnp.mean(x * x, axis=-1, keepdims=True) + 1e-06)
    return (x * scale * gain).astype(BF)


def gelu(x):
    return 0.5 * x * (1.0 + jnp.tanh(0.7978845608028654 * (x + 0.044715 * x * x * x)))


def drift_tools(
    chunks, p, dp, mask, g1, g2, nb, wq, wk, wv, wo, wu, wd, kb, vb, qb, mb, att, h_send, h_recv
):
    _, nodes, width = nb[0].shape
    rows = nodes // chunks
    head = width // HEADS

    side = 2 * lax.rem(p, 2) - 1
    partner, outer, same, last = 2 - side, 2 + side, 2 + 2 * side, 2 - 2 * side

    def copy_rows(k, c, src, dst, off, sem):
        part = pl.ds(c * rows, rows)
        return pltpu.make_async_remote_copy(
            src_ref=nb[k].at[src, part],
            dst_ref=nb[k].at[dst, part],
            send_sem=h_send.at[k, sem, c],
            recv_sem=h_recv.at[k, dst, c],
            device_id=dp(off),
            device_id_type=MESH,
        )

    def sends(k, c):
        return (
            copy_rows(k, c, 2, partner, side, 1),
            copy_rows(k, c, 2, same, -2 * side, 2),
            copy_rows(k, c, 2, outer, -side, 0),
        )

    def hand_on(k, c):
        return copy_rows(k, c, outer, same, -side, 3)

    def publish(k, c, x):
        part = pl.ds(c * rows, rows)
        nb[k][2, part] = rms(x.astype(F32), g1[...])
        for send in sends(k, c):
            send.start()

    def relay(k, c):
        copy_rows(k, c, 2, outer, side, 0).wait_recv()
        hand_on(k, c).start()

    def arrive(k, slot):
        for c in range(chunks):
            copy_rows(k, c, 2, slot, side, 0).wait_recv()

    def keys_values(k, slot):
        part = pl.ds(pl.multiple_of(slot * nodes, nodes), nodes)
        src = nb[k][slot]
        ks = dot(src, wk[...]).astype(BF)
        vs = dot(src, wv[...]).astype(BF)
        for h in range(HEADS):
            kb[h, part] = ks[:, h * head : (h + 1) * head]
            vb[h, part, pl.ds(0, head)] = vs[:, h * head : (h + 1) * head]

    def queries(k):
        qs = dot(nb[k][2], wq[...]).astype(BF)
        for h in range(HEADS):
            qb[h] = qs[:, h * head : (h + 1) * head]

    factor = 1.4426950408889634 / head**0.5
    span = 2 * REACH + 1

    def attend(b, h):
        kv = pl.ds(b * BLOCK, span * BLOCK)
        s = dot_nt(qb[h, pl.ds(b * BLOCK, BLOCK)], kb[h, kv]) * factor
        parts = []
        for i in range(span):
            piece = s[:, i * BLOCK : (i + 1) * BLOCK]
            if i != REACH:
                link = mask[b, i if i < REACH else i - 1]
                piece = piece + jnp.where(link > 0, F32(0.0), F32(-jnp.inf))
            parts.append(piece)
        s = jnp.concatenate(parts, axis=1)
        top = jnp.max(s, axis=1, keepdims=True)
        e = jnp.exp2(s - top)
        total = jnp.sum(e, axis=1, keepdims=True)
        mixed = dot(e.astype(BF), vb[h, kv, pl.ds(0, head)]) / total
        mb[pl.ds(b * BLOCK, BLOCK), pl.ds(pl.multiple_of(h * head, head), head)] = mixed.astype(BF)

    def attend_all(h):
        s = dot_nt(qb[h], kb[h]) * factor
        probs = []
        for b in range(nodes // BLOCK):
            parts = []
            for i in range(span):
                piece = s[b * BLOCK : (b + 1) * BLOCK, (b + i) * BLOCK : (b + i + 1) * BLOCK]
                if i != REACH:
                    link = mask[b, i if i < REACH else i - 1]
                    piece = piece + jnp.where(link > 0, F32(0.0), F32(-jnp.inf))
                parts.append(piece)
            sb = jnp.concatenate(parts, axis=1)
            e = jnp.exp2(sb - jnp.max(sb, axis=1, keepdims=True)).astype(BF)
            blank = jnp.zeros((BLOCK, BLOCK), BF)
            probs.append(jnp.concatenate([blank] * b + [e] + [blank] * (nodes // BLOCK - 1 - b), axis=1))
        both = dot(jnp.concatenate(probs, axis=0), vb[h])
        mixed = both[:, :head] / both[:, head:]
        mb[:, pl.ds(pl.multiple_of(h * head, head), head)] = mixed.astype(BF)

    def finish(state, part=slice(None)):
        att[part] = dot(mb[part], wo[...])
        lifted = state[part].astype(F32) + att[part]
        hidden = gelu(dot(rms(lifted, g2[...]), wu[...])).astype(BF)
        return (att[part] + dot(hidden, wd[...])).astype(BF)

    def h_drain():
        for k in range(2):
            for c in range(chunks):
                for send in sends(k, c) + (hand_on(k, c),):
                    send.wait_send()

    return (partner, outer, same, last), publish, relay, arrive, keys_values, queries, attend, attend_all, finish, h_drain


def ring_kernel(members, patches, *refs):
    (cb, ca, mask, e_in, f_in, g1, g2, wq_in, wk_in, wv_in, wo_in, wu_in, wd_in, out) = refs[:14]
    scratch = list(refs[14:])
    zb = [[scratch.pop(0) for _ in range(CHUNKS)] for _ in range(2)]
    nb = [scratch.pop(0) for _ in range(2)]
    wq, wk, wv, wo, wu, wd = [scratch.pop(0) for _ in range(6)]
    kb, vb, qb, mb, st, first, att, fx = [scratch.pop(0) for _ in range(8)]
    w_sem, own_sem, z_send, z_recv, h_send, h_recv = scratch

    z = lax.axis_index("member")
    p = lax.axis_index("patch")
    nodes, width = st.shape
    rows = nodes // CHUNKS
    head = width // HEADS
    right_ages = members // 2
    left_ages = members - 1 - right_ages

    def dz(off):
        return {"member": lax.rem(z + off + members, members)}

    def dp(off):
        return {"patch": lax.rem(p + off + patches, patches)}

    w_copies = [
        pltpu.make_async_copy(s, d, w_sem.at[i])
        for i, (s, d) in enumerate(zip((wq_in, wk_in, wv_in, wo_in, wu_in, wd_in), (wq, wk, wv, wo, wu, wd)))
    ]
    own = [
        [
            pltpu.make_async_copy(src.at[0, pl.ds(c * rows, rows)], zb[g][c].at[0], own_sem.at[g, c])
            for c in range(CHUNKS)
        ]
        for g, src in enumerate((e_in, f_in))
    ]
    for g in range(2):
        for c in range(CHUNKS):
            own[g][c].start()
    for w in w_copies:
        w.start()

    barrier = pltpu.get_barrier_semaphore()
    peers = [dz(1), dz(-1), dp(1), dp(-1), dp(2), dp(-2)]
    for peer in peers:
        pl.semaphore_signal(barrier, inc=1, device_id=peer, device_id_type=MESH)
    pl.semaphore_wait(barrier, len(peers))

    def ring(g, c, way, age):
        if way == 0:
            src, dst = age, age + 1
        else:
            src, dst = lax.rem(members - age, members), members - 1 - age
        return pltpu.make_async_remote_copy(
            src_ref=zb[g][c].at[src],
            dst_ref=zb[g][c].at[dst],
            send_sem=z_send.at[g, c, way],
            recv_sem=z_recv.at[g, c, way, age],
            device_id=dz(1 if way == 0 else -1),
            device_id_type=MESH,
        )

    def z_first(g):
        for c in range(CHUNKS):
            own[g][c].wait()
            ring(g, c, 0, 0).start()
            ring(g, c, 1, 0).start()

    def z_step(g, age, chunks):
        for c in chunks:
            ring(g, c, 0, age - 1).wait_recv()
            ring(g, c, 0, age).start()
            ring(g, c, 1, age - 1).wait_recv()
            ring(g, c, 1, age).start()

    def z_last(g, chunks):
        for c in chunks:
            ring(g, c, 0, right_ages - 2).wait_recv()
            ring(g, c, 0, right_ages - 1).start()
            ring(g, c, 1, left_ages - 1).wait_recv()

    def z_end(g, c):
        ring(g, c, 0, right_ages - 1).wait_recv()

    def z_drain():
        for g in range(2):
            for c in range(CHUNKS):
                for way, ages in ((0, right_ages), (1, left_ages)):
                    part = zb[g][c].at[pl.ds(0, ages)]
                    pltpu.make_async_remote_copy(
                        src_ref=part,
                        dst_ref=part,
                        send_sem=z_send.at[g, c, way],
                        recv_sem=z_recv.at[g, c, way, 0],
                        device_id=dz(1 if way == 0 else -1),
                        device_id_type=MESH,
                    ).wait_send()

    slots, publish, relay, arrive, keys_values, queries, attend, _, finish, h_drain = drift_tools(
        CHUNKS, p, dp, mask, g1, g2, nb, wq, wk, wv, wo, wu, wd, kb, vb, qb, mb, att, h_send, h_recv
    )

    z_first(0)

    @pl.loop(1, left_ages)
    def _(age):
        z_step(0, age, range(CHUNKS))

    z_last(0, range(CHUNKS))
    z_first(1)

    d_e = lax.rem(z - cb[ca[z]] + members, members)
    d_f = lax.rem(z - ca[z] + members, members)
    for c in range(CHUNKS):
        z_end(0, c)
        part = pl.ds(c * rows, rows)
        x = zb[0][c][d_e]
        st[part] = x
        publish(0, c, x)
    for w in w_copies:
        w.wait()
    queries(0)
    keys_values(0, 2)
    z_step(1, 1, range(CHUNKS))
    partner, outer, same, last = slots
    for c in range(CHUNKS):
        relay(0, c)
    arrive(0, partner)
    keys_values(0, partner)
    keys_values(0, outer)
    z_step(1, 2, range(CHUNKS))
    for slot in (same, last):
        arrive(0, slot)
        keys_values(0, slot)

    half = CHUNKS // 2

    @pl.loop(0, HEADS)
    def _(h):
        attend(0, h)

        @pl.when(h < HEADS - 1)
        def _():
            z_step(1, 3 + h, range(half))

        attend(1, h)

        @pl.when(h < HEADS - 1)
        def _():
            z_step(1, 3 + h, range(half, CHUNKS))

    first[...] = finish(st)

    @pl.loop(3 + HEADS - 1, left_ages)
    def _(age):
        z_step(1, age, range(CHUNKS))

    z_last(1, range(CHUNKS))
    for c in range(CHUNKS):
        z_end(1, c)
        part = pl.ds(c * rows, rows)
        base = st[part].astype(F32) + 0.3 * zb[1][c][d_f].astype(F32)
        x = (base + 0.5 * first[part].astype(F32)).astype(BF)
        fx[part] = x
        publish(1, c, x)
    queries(1)
    keys_values(1, 2)
    for c in range(CHUNKS):
        relay(1, c)
    arrive(1, partner)
    keys_values(1, partner)
    keys_values(1, outer)
    for slot in (same, last):
        arrive(1, slot)
        keys_values(1, slot)

    @pl.loop(0, HEADS)
    def _(h):
        attend(0, h)
        attend(1, h)

    second = finish(fx).astype(F32)
    for c in range(CHUNKS):
        part = pl.ds(c * rows, rows)
        base = st[part].astype(F32)
        tot = first[part].astype(F32) + second[c * rows : (c + 1) * rows]
        out[0, part] = (base + 0.25 * tot + 0.3 * zb[1][c][d_f].astype(F32)).astype(BF)

    h_drain()
    z_drain()


def thresholds(shape, members, g):
    q = lax.broadcasted_iota(jnp.int32, shape, 0)
    s = lax.rem(lax.broadcasted_iota(jnp.int32, shape, 1), members)
    x = (q * 40503 + s * 30011 + (g * 12289 + 7)) & 0xFFFF
    x = (x * 25173 + 13849) & 0xFFFF
    x = x ^ (x >> 7)
    x = (x * 25173 + 13849) & 0xFFFF
    x = x ^ (x >> 9)
    half = members // 2
    low = members - HOPS
    wide = low + ((x * (HOPS - low + 1)) >> 16)
    near = half - 1 + ((x * 2) >> 16)
    return jnp.where(q == 0, half, jnp.where(q == 1, half - 1, jnp.where(q < shape[0] // 4, near, wide)))


def make_plan(members, z, sources, starts, plan):
    shape = starts.shape[2:]
    lane = lax.broadcasted_iota(jnp.int32, shape, 1)
    slot = lax.rem(lane, members)
    zero = jnp.zeros(shape, jnp.int32)
    reach = []
    for g in range(2):
        src = zero
        for m in range(members):
            src = jnp.where(slot == m, sources[g][m], src)
        dist = lax.rem(slot - src + members, members)
        right = dist <= thresholds(shape, members, g)
        away = (jnp.where(right, dist, 0), jnp.where(right, 0, members - dist))
        both = []
        for way in range(2):
            far = zero
            for b in range(1, HOPS + 1):
                shift = (128 - b) if way == 0 else b
                far = jnp.where(pltpu.roll(away[way], shift, 1) == b, b, far)
            both.append(far)
        reach.append(both)
    free = [zero, zero]
    ends = [zero, zero]
    before = [[None, None], [None, None]]
    for g, a in sorted(((g, a) for g in range(2) for a in range(HOPS)), key=lambda hop: (hop[1] + BEHIND * hop[0], hop[0])):
        for way in range(2):
            sgn = 1 if way == 0 else 127
            far = reach[g][way]
            if a > 0:
                far = pltpu.roll(far, a if way == 0 else 128 - a, 1)
            need = far > a
            t = free[way]
            if a > 0:
                t = jnp.maximum(t, pltpu.roll(before[g][way], sgn, 1) + LAG)
            free[way] = jnp.where(need, t + PIECES, free[way])
            ends[g] = jnp.maximum(ends[g], jnp.where(need, t + PIECES, 0))
            before[g][way] = jnp.where(need, t, -4096)
            starts[way, g * HOPS + a] = before[g][way]
    ends = [jnp.max(end, axis=1, keepdims=True) for end in ends]
    late = jnp.maximum(ends[0] - MID, ends[1] - STEPS)
    late = jnp.broadcast_to(late, shape)
    key = late * PLANS + lax.broadcasted_iota(jnp.int32, shape, 0)
    best = jnp.min(key, axis=0, keepdims=True)
    picked = key == best
    fits = jnp.where(best < PLANS, 1, 0)

    items = 2 * HOPS
    lane1 = lax.broadcasted_iota(jnp.int32, (1, 128), 1)
    sent, came = [], []
    for way in range(2):
        from_lane = lax.rem(z + members - 1, members) if way == 0 else lax.rem(z + 1, members)
        mine, theirs = [], []
        for r in range(items):
            row = jnp.sum(jnp.where(picked, starts[way, r], 0), axis=0, keepdims=True)
            mine.append(jnp.broadcast_to(jnp.sum(jnp.where(lane1 == z, row, 0), axis=1, keepdims=True), (1, 128)))
            theirs.append(
                jnp.broadcast_to(jnp.sum(jnp.where(lane1 == from_lane, row, 0), axis=1, keepdims=True), (1, 128))
            )
        sent.append(mine)
        came.append(theirs)
    top = 2 * PIECES + 2 * STEPS
    rows = []
    for way in range(2):
        base = 2 * PIECES + way * STEPS
        index = jnp.zeros((1, 128), jnp.int32)
        for g in range(2):
            for a in range(HOPS):
                at = sent[way][g * HOPS + a]
                first = g * PIECES if a == 0 else base + came[way][g * HOPS + a - 1]
                hit = (lane1 >= at) & (lane1 < at + PIECES)
                index = jnp.where(hit, first + lane1 - at, index)
        rows.append(jnp.clip(index, 0, top - 1))
    return rows, came, fits, lane1, top


def route_kernel(members, patches, *refs):
    (cb, ca, mask, e_in, f_in, g1, g2, wq_in, wk_in, wv_in, wo_in, wu_in, wd_in, out, fine) = refs[:15]
    scratch = list(refs[15:])
    nb = [scratch.pop(0) for _ in range(2)]
    wq, wk, wv, wo, wu, wd = [scratch.pop(0) for _ in range(6)]
    kb, vb, qb, mb, st, first, att, fx = [scratch.pop(0) for _ in range(8)]
    pool, staged, landed, starts, plan, table = [scratch.pop(0) for _ in range(6)]
    w_sem, own_sem, plan_sem, z_send, z_recv, h_send, h_recv = scratch

    z = lax.axis_index("member")
    p = lax.axis_index("patch")
    nodes, width = st.shape
    rows = nodes // PIECES

    def dz(off):
        return {"member": lax.rem(z + off + members, members)}

    def dp(off):
        return {"patch": lax.rem(p + off + patches, patches)}

    own = [
        pltpu.make_async_copy(src.at[0, pl.ds(c * rows, rows)], pool.at[g * PIECES + c], own_sem.at[g, c])
        for g, src in enumerate((e_in, f_in))
        for c in range(PIECES)
    ]
    for copy in own:
        copy.start()
    w_copies = [
        pltpu.make_async_copy(s, d, w_sem.at[i])
        for i, (s, d) in enumerate(zip((wq_in, wk_in, wv_in, wo_in, wu_in, wd_in), (wq, wk, wv, wo, wu, wd)))
    ]
    for w in w_copies:
        w.start()
    barrier = pltpu.get_barrier_semaphore()
    peers = [dz(1), dz(-1), dp(1), dp(-1), dp(2), dp(-2)]
    for peer in peers:
        pl.semaphore_signal(barrier, inc=1, device_id=peer, device_id_type=MESH)

    moved = [ca[s] for s in range(members)]
    sources = ([cb[m] for m in moved], moved)
    index, came, fits, lane1, top = make_plan(members, z, sources, starts, plan)
    mine = ca[z]
    finals = []
    for g, src in enumerate((cb[mine], mine)):
        dist = lax.rem(z - src + members, members)
        at = jnp.full((1, 128), g * PIECES, jnp.int32)
        for way in (1, 0):
            gone = dist if way == 0 else members - dist
            for a in range(HOPS):
                begin = came[way][g * HOPS + a]
                use = (begin >= 0) & (gone == a + 1)
                at = jnp.where(use, 2 * PIECES + way * STEPS + begin, at)
        finals.append(jnp.clip(at, 0, top - PIECES))
    plan[...] = jnp.zeros(plan.shape, jnp.int32)
    for r, row in enumerate((index[0], index[1], finals[0], finals[1], fits)):
        plan[pl.ds(r, 1)] = row
    to_smem = pltpu.make_async_copy(plan, table, plan_sem)
    to_smem.start()
    for h in range(HEADS):
        vb[h, :, pl.ds(width // HEADS, width // HEADS)] = jnp.ones((vb.shape[1], width // HEADS), BF)
    for copy in own:
        copy.wait()
    pl.semaphore_wait(barrier, len(peers))
    to_smem.wait()
    fine[0, 0] = table[4, 0]

    def hop(way, t):
        return pltpu.make_async_remote_copy(
            src_ref=staged.at[way, t],
            dst_ref=landed.at[way, t],
            send_sem=z_send.at[way],
            recv_sem=z_recv.at[way, t],
            device_id=dz(1 if way == 0 else -1),
            device_id_type=MESH,
        )

    def take(t, way):
        hop(way, t).wait_recv()
        pool[2 * PIECES + way * STEPS + t] = landed[way, t]

    def give(t, way):
        staged[way, t] = pool[table[way, t]]
        hop(way, t).start()

    def step(t):
        for way in range(2):
            take(t - LAG, way)
            give(t, way)

    def piece(g, c):
        return pool[table[2 + g, 0] + c]

    slots, publish, relay, arrive, keys_values, queries, attend, attend_all, finish, h_drain = drift_tools(
        PIECES, p, dp, mask, g1, g2, nb, wq, wk, wv, wo, wu, wd, kb, vb, qb, mb, att, h_send, h_recv
    )

    for t in range(LAG):
        for way in range(2):
            give(t, way)

    @pl.loop(LAG, MID - PIECES + LAG)
    def _(t):
        step(t)

    partner, outer, same, last = slots
    delay = 5
    for c in range(PIECES):
        step(MID - PIECES + LAG + c)
        x = piece(0, c)
        st[pl.ds(c * rows, rows)] = x
        publish(0, c, x)
        if c >= delay:
            relay(0, c - delay)
    for w in w_copies:
        w.wait()
    now = MID + LAG
    queries(0)
    step(now)
    relay(0, PIECES - delay)
    keys_values(0, 2)
    step(now + 1)
    relay(0, PIECES - delay + 1)
    arrive(0, partner)
    step(now + 2)
    relay(0, PIECES - delay + 2)
    keys_values(0, partner)
    step(now + 3)
    relay(0, PIECES - delay + 3)
    step(now + 4)
    relay(0, PIECES - delay + 4)
    keys_values(0, outer)
    now += 5
    for slot, count in ((same, 2), (last, 2)):
        arrive(0, slot)
        keys_values(0, slot)
        for t in range(now, now + count):
            step(t)
        now += count
    for t in range(now, STEPS):
        step(t)

    blocks = nodes // BLOCK
    for b in range(blocks):
        for h in range(HEADS):
            attend(b, h)
        half = pl.ds(b * BLOCK, BLOCK)
        first[half] = finish(st, half)
        for c in range(b * PIECES // blocks, (b + 1) * PIECES // blocks):
            t = STEPS - PIECES + c
            if t >= STEPS - LAG:
                for way in range(2):
                    take(t, way)
            part = pl.ds(c * rows, rows)
            base = st[part].astype(F32) + 0.3 * piece(1, c).astype(F32)
            x = (base + 0.5 * first[part].astype(F32)).astype(BF)
            fx[part] = x
            publish(1, c, x)
    queries(1)
    keys_values(1, 2)
    for c in range(PIECES // 2):
        relay(1, c)
    arrive(1, partner)
    keys_values(1, partner)
    for c in range(PIECES // 2, PIECES):
        relay(1, c)
    keys_values(1, outer)
    for slot in (same, last):
        arrive(1, slot)
        keys_values(1, slot)

    for h in range(HEADS):
        attend_all(h)

    second = finish(fx).astype(F32)
    for c in range(PIECES):
        part = pl.ds(c * rows, rows)
        base = st[part].astype(F32)
        tot = first[part].astype(F32) + second[c * rows : (c + 1) * rows]
        out[0, part] = (base + 0.25 * tot + 0.3 * piece(1, c).astype(F32)).astype(BF)

    h_drain()
    for way in range(2):
        pltpu.make_async_remote_copy(
            src_ref=staged.at[way],
            dst_ref=landed.at[way],
            send_sem=z_send.at[way],
            recv_sem=z_recv.at[way, 0],
            device_id=dz(1 if way == 0 else -1),
            device_id_type=MESH,
        ).wait_send()


def solution(mesh):
    members, patches = mesh.shape["member"], mesh.shape["patch"]

    def shards(ensemble, forcing, cb, ca, mask, g1, wq, wk, wv, wo, g2, wu, wd):
        _, nodes, width = ensemble.shape
        hidden = wu.shape[1]
        rows = nodes // CHUNKS
        head = width // HEADS
        smem = pl.BlockSpec(memory_space=pltpu.SMEM)
        vmem = pl.BlockSpec(memory_space=pltpu.VMEM)
        anym = pl.BlockSpec(memory_space=pl.ANY)
        state = jax.ShapeDtypeStruct(ensemble.shape, BF)
        common = (
            [pltpu.VMEM((5, nodes, width), BF) for _ in range(2)]
            + [pltpu.VMEM((width, width), BF) for _ in range(4)]
            + [pltpu.VMEM((width, hidden), BF), pltpu.VMEM((hidden, width), BF)]
            + [pltpu.VMEM((HEADS, 5 * nodes, head), BF), pltpu.VMEM((HEADS, 5 * nodes, 2 * head), BF)]
            + [pltpu.VMEM((HEADS, nodes, head), BF)]
            + [pltpu.VMEM((nodes, width), BF) for _ in range(3)]
            + [pltpu.VMEM((nodes, width), F32), pltpu.VMEM((nodes, width), BF)]
        )
        dma = pltpu.SemaphoreType.DMA

        def params(cid):
            return pltpu.CompilerParams(
                collective_id=cid, has_side_effects=True, vmem_limit_bytes=56 * 1024 * 1024
            )

        ins = [smem] * 3 + [anym] * 2 + [vmem] * 2 + [anym] * 6
        args = (cb, ca, mask, ensemble, forcing, g1.reshape(1, width), g2.reshape(1, width), wq, wk, wv, wo, wu, wd)
        size = nodes // PIECES
        out, fine = pl.pallas_call(
            functools.partial(route_kernel, members, patches),
            out_shape=(state, jax.ShapeDtypeStruct((1, 1), jnp.int32)),
            in_specs=ins,
            out_specs=(vmem, smem),
            scratch_shapes=common
            + [
                pltpu.VMEM((2 * PIECES + 2 * STEPS, size, width), BF),
                pltpu.VMEM((2, STEPS, size, width), BF),
                pltpu.VMEM((2, STEPS, size, width), BF),
                pltpu.VMEM((2, 2 * HOPS, PLANS, 128), jnp.int32),
                pltpu.VMEM((8, 128), jnp.int32),
                pltpu.SMEM((8, 128), jnp.int32),
                dma((6,)),
                dma((2, PIECES)),
                dma,
                dma((2,)),
                dma((2, STEPS)),
                dma((2, 5, PIECES)),
                dma((2, 5, PIECES)),
            ],
            compiler_params=params(0),
            name="route",
        )(*args)

        def slow(_):
            return pl.pallas_call(
                functools.partial(ring_kernel, members, patches),
                out_shape=state,
                in_specs=ins,
                out_specs=vmem,
                scratch_shapes=[pltpu.VMEM((members, rows, width), BF) for _ in range(2 * CHUNKS)]
                + common
                + [
                    dma((6,)),
                    dma((2, CHUNKS)),
                    dma((2, CHUNKS, 2)),
                    dma((2, CHUNKS, 2, members // 2)),
                    dma((2, 5, CHUNKS)),
                    dma((2, 5, CHUNKS)),
                ],
                compiler_params=params(1),
                name="ring",
            )(*args)

        return lax.cond(fine[0, 0] > 0, lambda x: x, slow, out)

    placed = (P("member", "patch", None),) * 2 + (P(), P(), P("patch", None)) + (P(),) * 8
    return jax.shard_map(
        shards, mesh=mesh, in_specs=placed, out_specs=P("member", "patch", None), check_vma=False
    )
```
